32 devices in a mesh: hist: 4 (over y, x), tcol: 8 (over z, core).
Axes of the slice: x: 2, y: 2, z: 4, core: 2. Of those that a mesh axis runs over, the one named last changes fastest.
Arguments:
- history: float32 [8192, 4096], P('hist', 'tcol'), may hold values from -5 to 5
- memory_weight_first: float32 [512, 8192], P(None, 'hist'), may hold values from -0.09375 to 0.09375
- memory_weight_second: float32 [512, 8192], P(None, 'hist'), may hold values from -0.09375 to 0.09375
- link: float32 [512, 512], replicated, may hold values from -0.25 to 0.25
- propagator: float32 [4096, 4096], P(None, 'tcol'), may hold values from -0.09375 to 0.09375
- inverse_one: float32 [512, 512], replicated, as said below
- inverse_two: float32 [512, 512], replicated, as said below
- explicit_first: float32 [512, 4096], P(None, 'tcol'), may hold values from -5 to 5
- explicit_second: float32 [512, 4096], P(None, 'tcol'), may hold values from -5 to 5
Outputs:
- first_slab_rows: float32 [512, 4096], P('hist', 'tcol')
- slab_two: float32 [512, 4096], P('hist', 'tcol')
The draws below stay inside these ranges and needn't reach their ends.
Inputs may be any that keep to these rules, and one draw needn't show every extreme that they name: `inverse_one`: the identity plus independent entries of deviation 0.5 / sqrt(512). `inverse_two`: the identity plus independent entries of deviation 0.5 / sqrt(512).
All inputs are finite; a program needn't handle non-finite values.
Results may differ from the reference program's by a relative error of at most 0.0003.
Values sent between devices are 32-bit elements; how exact they have to be, the bound alone decides.
A program may use at most 128 MiB of HBM per device.

```python
import jax
import jax.numpy as jnp
from jax import lax

S = 512
HT = 8192
NC = 4096


def inverse_common(key, salt):
    sub = jax.random.fold_in(key, salt)
    noise = jax.random.normal(sub, (S, S), jnp.float32)
    return jnp.eye(S, dtype=jnp.float32) + noise * (0.5 / jnp.sqrt(jnp.float32(S)))


def draw_inverse_one(key, part):
    return inverse_common(key, 101)


def draw_inverse_two(key, part):
    return inverse_common(key, 202)


def strengthened(values, stream_key, source, target, parts, factor):
    owner, partner = [(jnp.arange(values.shape[position]) // (values.shape[position] // parts)).reshape([-1 if axis == position else 1 for axis in range(values.ndim)]) for position in (source, target)]
    chosen = jax.random.permutation(stream_key, parts)[partner]
    strong = (owner == chosen) | (owner == (partner + parts // 2) % parts)
    return jnp.where(strong, factor * values, values)


def levels(own_key, extent, split, low, high):
    def one(position, shards_of):
        draws = jax.random.uniform(jax.random.fold_in(jax.random.fold_in(own_key, 6), position), (shards_of,), jnp.float32, low / len(split), high / len(split))
        return jnp.repeat(jnp.exp(draws), extent[position] // shards_of).reshape((-1,) + (1,) * (len(extent) - position - 1))

    loudness = one(*split[0])
    for cut in split[1:]:
        loudness = loudness * one(*cut)
    return loudness


def gaussian(rng, shape, deviation, limit, pieces=(), held_as=jnp.bfloat16):
    level = levels(rng, shape, pieces, -0.22, 0.18) if pieces else 1.0
    drawn = jax.random.normal(rng, shape, jnp.float32) * deviation * level
    return jnp.minimum(jnp.maximum(drawn, -limit), limit).astype(held_as)


def heavy_noise(key, shape, spread, reach, cuts, heavy, kind=jnp.bfloat16):
    result = spread * jax.random.normal(key, shape, jnp.float32)
    if cuts:
        result = result * levels(key, shape, cuts, -0.22, 0.18)
    return jnp.clip(strengthened(result, jax.random.fold_in(key, 3), *heavy), -reach, reach).astype(kind)


def setup_inputs(seed: int = 0) -> dict:
    key_list = jax.random.split(jax.random.key(seed), 10)
    return {
        "history": gaussian(key_list[0], (HT, NC), 0.8, 5.0, ((0, 4), (1, 8)), jnp.float32),
        "memory_weight_first": heavy_noise(key_list[1], (S, HT), HT ** -0.5, 0.09375, ((1, 4),), (1, 0, 4, 2.0), jnp.float32),
        "memory_weight_second": heavy_noise(key_list[2], (S, HT), HT ** -0.5, 0.09375, ((1, 4),), (1, 0, 4, 2.0), jnp.float32),
        "link": gaussian(key_list[3], (S, S), S ** -0.5, 0.25, (), jnp.float32),
        "propagator": gaussian(key_list[4], (NC, NC), NC ** -0.5, 0.09375, ((1, 8),), jnp.float32),
        "inverse_one": draw_inverse_one(jax.random.fold_in(key_list[9], 71), 0),
        "inverse_two": draw_inverse_two(jax.random.fold_in(key_list[9], 71), 0),
        "explicit_first": gaussian(key_list[7], (S, NC), 0.7, 5.0, ((1, 8),), jnp.float32),
        "explicit_second": gaussian(key_list[8], (S, NC), 0.7, 5.0, ((1, 8),), jnp.float32),
    }


strength = 0.2
step_size = 0.5
highest = lax.Precision.HIGHEST


def cubic_power(value):
    return strength * value * value * value


def matrix_product(left, right):
    return jnp.dot(left, right, preferred_element_type=jnp.float32, precision=highest)


def reference(history, memory_weight_first, memory_weight_second, link, propagator, inverse_one, inverse_two, explicit_first, explicit_second):
    self_energy_history = cubic_power(history)
    predictor_first = explicit_first + matrix_product(memory_weight_first, self_energy_history)
    mem_one = matrix_product(cubic_power(predictor_first), propagator)
    first_slab_rows = matrix_product(inverse_one, predictor_first + step_size * mem_one)
    collision_second = matrix_product(memory_weight_second, self_energy_history) + matrix_product(link, cubic_power(first_slab_rows))
    predictor_second = explicit_second + collision_second
    mem_two = matrix_product(cubic_power(predictor_second), propagator)
    slab_two = matrix_product(inverse_two, predictor_second + step_size * mem_two)
    return first_slab_rows, slab_two
```

```python
import functools

import jax
import jax.numpy as jnp
from jax import lax
from jax.experimental import pallas as pl
from jax.experimental.pallas import tpu as pltpu
from jax.sharding import PartitionSpec as P

strength = 0.2
step_size = 0.5
MESH = pl.DeviceIdType.MESH
f32 = jnp.float32
bf16 = jnp.bfloat16


def cubic_power(value):
    return strength * value * value * value


def halves(value):
    high = value.astype(bf16)
    return high, (value - high.astype(f32)).astype(bf16)


def mm(left, right):
    return jnp.dot(left, right, preferred_element_type=f32)


def product(left, right_high, right_low):
    m = left.shape[0]
    high, low = halves(left)
    both = mm(jnp.concatenate([high, low], axis=0), right_high)
    return both[:m] + both[m:] + mm(high, right_low)


def kernel(
    H, T, C,
    hist_ref, w1_ref, w2_ref, link_ref, prop_ref, inv1_ref, inv2_ref, e1_ref, e2_ref,
    o1_ref, o2_ref,
    hbuf, wbuf, wh, wl, sh, sl, ph, plo, mat, ih, il, kh, kl, vh, vl, e1, e2,
    part, rs, pred, acc1, acc2, g1, g2, nsend, nrecv, near, rsend, rf, s1, s2, orecv,
    ysend, yrecv, bsend, brecv, xh, xl, p2h, p2l, qh, ql,
    hsem, wsem, psem, msem, rs_send, rs_recv, x_sent, x_got,
    sp, sr, sleft, rz, rp,
):
    K, N = hist_ref.shape
    S = w1_ref.shape[0]
    R = S // H
    Rc = R // C
    Nh = N // H
    nK = K // N
    Z = T // 2
    h = lax.axis_index("hist")
    t = lax.axis_index("tcol")
    p = t // 2
    core = t % 2
    other = 1 - core
    tile = 32

    def split(source, high, low, rows, function=lambda v: v):
        @pl.loop(0, rows // tile)
        def _(i):
            at = pl.ds(pl.multiple_of(i * tile, tile), tile)
            a, b = halves(function(source[at, :]))
            high[at, :] = a
            low[at, :] = b

    def hist_copy(kb):
        return pltpu.make_async_copy(hist_ref.at[pl.ds(kb * N, N), :], hbuf.at[kb], hsem.at[kb])

    def w_copy(w, c, j):
        ref = (w1_ref, w2_ref)[w]
        return pltpu.make_async_copy(
            ref.at[pl.ds(j * R + c * Rc, Rc), :], wbuf.at[w, c, j], wsem.at[w, c, j]
        )

    def p_copy(b):
        return pltpu.make_async_copy(
            prop_ref.at[pl.ds(b * N, N), :], hbuf.at[b % nK], psem.at[b]
        )

    own_rows = pl.ds(pl.multiple_of(h * R, R), R)
    small = (
        pltpu.make_async_copy(e1_ref.at[own_rows, :], e1, msem.at[0]),
        pltpu.make_async_copy(inv1_ref, mat.at[0], msem.at[1]),
        pltpu.make_async_copy(link_ref, mat.at[1], msem.at[2]),
        pltpu.make_async_copy(inv2_ref, mat.at[2], msem.at[3]),
        pltpu.make_async_copy(e2_ref.at[own_rows, :], e2, msem.at[4]),
    )

    for kb in range(nK):
        hist_copy(kb).start()
    for c in range(C):
        for j in range(H):
            w_copy(0, c, j).start()
    small[0].start()

    barrier = pltpu.get_barrier_semaphore()

    def greet(device):
        pl.semaphore_signal(barrier, inc=1, device_id=device, device_id_type=MESH)

    for d in range(1, H):
        greet({"hist": lax.rem(h + d, H)})
    greet({"tcol": p * 2 + other})

    greet({"tcol": lax.rem(p + 1, Z) * 2 + core})
    greet({"tcol": lax.rem(p + Z - 1, Z) * 2 + core})

    for kb in range(nK):
        hist_copy(kb).wait()
        split(hbuf.at[kb], sh.at[kb], sl.at[kb], N, cubic_power)

    for c in range(C):
        for j in range(H):
            w_copy(1, c, j).start()
    for copy in small[1:]:
        copy.start()
    for b in range(nK):
        p_copy(b).start()

    def history_sum(w, c):
        for j in range(H):
            w_copy(w, c, j).wait()
            split(wbuf.at[w, c, j], wh.at[j], wl.at[j], Rc)

        for kb in range(nK):
            cols = pl.ds(kb * N, N)
            a = wh[:, :, cols].reshape(H * Rc, N)
            b = wl[:, :, cols].reshape(H * Rc, N)
            value = mm(a, sh[kb]) + mm(b, sh[kb]) + mm(a, sl[kb])
            value = value.reshape(H, Rc, N)
            if kb == 0:
                part[w, c] = value
            else:
                part[w, c] += value

    def rs_copy(c, d):
        dst = lax.rem(h + d, H)
        return pltpu.make_async_remote_copy(
            src_ref=part.at[0, c, dst], dst_ref=rs.at[c, d - 1],
            send_sem=rs_send.at[c, d - 1], recv_sem=rs_recv.at[c, d - 1],
            device_id={"hist": dst}, device_id_type=MESH,
        )

    def gathered(c):
        total = part[0, c, h]
        for d in range(1, H):
            rs_copy(c, d).wait_recv()
            total += rs[c, d - 1]
        return total

    def exchange(kind, d, source, target):
        dst = lax.rem(h + d, H)
        return pltpu.make_async_remote_copy(
            src_ref=source(dst), dst_ref=target(h, d),
            send_sem=x_sent.at[kind, d - 1], recv_sem=x_got.at[kind, d - 1],
            device_id={"hist": dst}, device_id_type=MESH,
        )

    def arrived(kind, d, target):
        src = lax.rem(h + H - d, H)
        ref = target(src, d)
        pltpu.make_async_remote_copy(
            src_ref=ref, dst_ref=ref,
            send_sem=x_sent.at[kind, d - 1], recv_sem=x_got.at[kind, d - 1],
            device_id={"hist": src}, device_id_type=MESH,
        ).wait_recv()

    plans = {}
    for c in range(C):
        plans[c] = (
            lambda dst, c=c: nsend.at[c, dst], lambda src, d, c=c: nrecv.at[c, d - 1])
        plans[C + c] = (
            lambda dst, c=c: rsend.at[c, dst], lambda src, d, c=c: rf.at[c, src])
        plans[2 * C + c] = (
            lambda dst, c=c: ysend.at[c, dst], lambda src, d, c=c: yrecv.at[c, src])
    plans[3 * C] = (lambda dst: s1.at[dst], lambda src, d: orecv.at[src])
    plans[3 * C + 1] = (lambda dst: bsend.at[dst], lambda src, d: brecv.at[src])

    def x_start(kind):
        for d in range(1, H):
            exchange(kind, d, *plans[kind]).start()

    def x_wait(kind):
        for d in range(1, H):
            arrived(kind, d, plans[kind][1])

    def z_copy(g, st, c, q, where):
        block = g.at[c, 2 * q + core]
        send, recv, target = {
            "partner": (sp, rp, p * 2 + other),
            "right": (sr, rz, t + 2),
            "left": (sleft, rz, t - 2),
        }[where]
        return pltpu.make_async_remote_copy(
            src_ref=block, dst_ref=block,
            send_sem=send.at[st, c, q], recv_sem=recv.at[st, c, q],
            device_id={"tcol": target}, device_id_type=MESH,
        )

    def z_partner_wait(g, st, c, q):
        block = g.at[c, 2 * q + other]
        pltpu.make_async_remote_copy(
            src_ref=block, dst_ref=block,
            send_sem=sp.at[st, c, q], recv_sem=rp.at[st, c, q],
            device_id={"tcol": p * 2 + other}, device_id_type=MESH,
        ).wait_recv()

    def z_own(g, st, c):
        @pl.when(p + 1 < Z)
        def _():
            z_copy(g, st, c, p, "right").start()

        @pl.when(p > 0)
        def _():
            z_copy(g, st, c, p, "left").start()

        z_copy(g, st, c, p, "partner").start()

    def z_step(g, st, c, s, use):
        @pl.when(p >= s)
        def _():
            q = p - s
            z_copy(g, st, c, q, "right").wait_recv()

            @pl.when(p + 1 < Z)
            def _():
                z_copy(g, st, c, q, "right").start()

            z_copy(g, st, c, q, "partner").start()

        @pl.when(p + s < Z)
        def _():
            q = p + s
            z_copy(g, st, c, q, "left").wait_recv()

            @pl.when(p > 0)
            def _():
                z_copy(g, st, c, q, "left").start()

            z_copy(g, st, c, q, "partner").start()

        @pl.when(p >= s)
        def _():
            use(c, 2 * (p - s) + core)

        @pl.when(p + s < Z)
        def _():
            use(c, 2 * (p + s) + core)

        @pl.when(p >= s)
        def _():
            z_partner_wait(g, st, c, p - s)
            use(c, 2 * (p - s) + other)

        @pl.when(p + s < Z)
        def _():
            z_partner_wait(g, st, c, p + s)
            use(c, 2 * (p + s) + other)

    def z_finish(g, st, c):
        z_copy(g, st, c, p, "partner").wait_send()

        @pl.when(p + 1 < Z)
        def _():
            z_copy(g, st, c, p, "right").wait_send()

        @pl.when(p > 0)
        def _():
            z_copy(g, st, c, p, "left").wait_send()

        for s in range(1, Z):
            @pl.when(p >= s)
            def _():
                z_copy(g, st, c, p - s, "partner").wait_send()

                @pl.when(p + 1 < Z)
                def _():
                    z_copy(g, st, c, p - s, "right").wait_send()

            @pl.when(p + s < Z)
            def _():
                z_copy(g, st, c, p + s, "partner").wait_send()

                @pl.when(p > 0)
                def _():
                    z_copy(g, st, c, p + s, "left").wait_send()

    def use_one(c, b):
        acc1[c] += product(g1[c, b], ph[b], plo[b])

    def use_two(c, b):
        acc2[c] += product(g2[c, b], ph[b], plo[b])

    history_sum(0, 0)
    pl.semaphore_wait(barrier, H + 2)

    for d in range(1, H):
        rs_copy(0, d).start()
    for c in range(1, C):
        history_sum(0, c)
        for d in range(1, H):
            rs_copy(c, d).start()

    small[0].wait()

    def begin_one(c):
        value = gathered(c) + e1[pl.ds(c * Rc, Rc), :]
        pred[c] = value
        g1[c, t] = cubic_power(value)
        z_own(g1, 0, c)

    for b in range(T):
        p_copy(b).wait()
        split(hbuf.at[b % nK], ph.at[b], plo.at[b], N)
        if b + nK < T:
            p_copy(b + nK).start()

    small[4].wait()

    def near_sums(c):
        history_sum(1, c)
        part[1, c, h] += e2[pl.ds(c * Rc, Rc), :]
        for j in range(H):
            nsend[c, j] = part[1, c, :, :, j * Nh:(j + 1) * Nh]
        x_start(c)

    def local_one(c):
        acc1[c] = product(g1[c, t], ph[t], plo[t])
        z_partner_wait(g1, 0, c, p)
        use_one(c, 2 * p + other)

    begin_one(0)
    near_sums(0)
    for c in range(1, C):
        begin_one(c)
    for c in range(C):
        local_one(c)
        z_step(g1, 0, c, 1, use_one)
    for c in range(1, C):
        near_sums(c)

    for copy in small[1:4]:
        copy.wait()
    split(mat.at[0], ih, il, S)
    split(mat.at[1], kh, kl, S)
    split(mat.at[2], vh, vl, S)

    def send_right(c):
        value = pred[c] + step_size * acc1[c]
        for j in range(H):
            rsend[c, j] = value[:, j * Nh:(j + 1) * Nh]
        x_start(C + c)
        rf[c, h] = rsend[c, h]

    def sum_near():
        for c in range(C):
            x_wait(c)
            total = nsend[c, h]
            for d in range(1, H):
                total += nrecv[c, d - 1]
            near[:, c] = total

    for s in range(2, Z):
        for c in range(C):
            z_step(g1, 0, c, s, use_one)
            if s == Z - 1:
                send_right(c)
    if Z == 2:
        for c in range(C):
            send_right(c)
    sum_near()

    for c in range(C):
        x_wait(C + c)

        @pl.loop(0, H)
        def _(j):
            a, b = halves(rf[c, j])
            xh[j, c] = a
            xl[j, c] = b

    def apply(high, low, j, a, b):
        rows = pl.ds(pl.multiple_of(j * R, R), R)
        left, rest = high[rows, :], low[rows, :]
        return mm(left, a) + mm(rest, a) + mm(left, b)

    a, b = xh[...].reshape(S, Nh), xl[...].reshape(S, Nh)

    @pl.loop(0, H)
    def _(j):
        value = apply(ih, il, j, a, b)
        s1[j] = value
        p2h[j], p2l[j] = halves(cubic_power(value))

    a, b = p2h[...].reshape(S, Nh), p2l[...].reshape(S, Nh)

    @pl.loop(0, H)
    def _(j):
        value = apply(kh, kl, j, a, b) + near[j].reshape(R, Nh)
        s2[j] = value
        qh[j], ql[j] = halves(step_size * cubic_power(value))

    a, b = qh[...].reshape(S, Nh), ql[...].reshape(S, Nh)

    @pl.loop(0, H)
    def _(j):
        value = apply(vh, vl, j, a, b)
        for c in range(C):
            ysend[c, j] = value[c * Rc:(c + 1) * Rc, :]

    for c in range(C):
        x_start(2 * C + c)
        yrecv[c, h] = ysend[c, h]
    x_start(3 * C)
    orecv[h] = s1[h]

    @pl.loop(0, H)
    def _(j):
        p2h[j], p2l[j] = halves(s2[j])

    a, b = p2h[...].reshape(S, Nh), p2l[...].reshape(S, Nh)

    @pl.loop(0, H)
    def _(j):
        bsend[j] = apply(vh, vl, j, a, b)

    def begin_two(c):
        x_wait(2 * C + c)
        g2[c, t] = jnp.concatenate([yrecv[c, j] for j in range(H)], axis=1)
        z_own(g2, 1, c)

    def local_two(c):
        acc2[c] = product(g2[c, t], ph[t], plo[t])
        z_partner_wait(g2, 1, c, p)
        use_two(c, 2 * p + other)

    for c in range(C):
        begin_two(c)
    x_start(3 * C + 1)
    brecv[h] = bsend[h]
    for c in range(C):
        local_two(c)
        z_step(g2, 1, c, 1, use_two)
    x_wait(3 * C)
    for j in range(H):
        o1_ref[:, j * Nh:(j + 1) * Nh] = orecv[j]
    for s in range(2, Z):
        for c in range(C):
            z_step(g2, 1, c, s, use_two)
    x_wait(3 * C + 1)
    for c in range(C):
        rows = pl.ds(c * Rc, Rc)
        o2_ref[rows, :] = acc2[c] + jnp.concatenate([brecv[j, rows, :] for j in range(H)], axis=1)

    for c in range(C):
        for d in range(1, H):
            rs_copy(c, d).wait_send()
        z_finish(g1, 0, c)
        z_finish(g2, 1, c)
    for kind in range(3 * C + 2):
        for d in range(1, H):
            exchange(kind, d, *plans[kind]).wait_send()


def shards(*operands):
    history, w1 = operands[:2]
    K, N = history.shape
    S = w1.shape[0]
    H, T, C = lax.axis_size("hist"), lax.axis_size("tcol"), 2
    R = S // H
    Rc, Nh, nK, Z = R // C, N // H, K // N, T // 2
    V, D = pltpu.VMEM, pltpu.SemaphoreType.DMA
    return pl.pallas_call(
        functools.partial(kernel, H, T, C),
        out_shape=[pltpu.VMEM((R, N), f32)] * 2,
        in_specs=[pl.BlockSpec(memory_space=pl.ANY)] * 9,
        out_specs=[pl.BlockSpec(memory_space=pltpu.VMEM)] * 2,
        scratch_shapes=[
            V((nK, N, N), f32), V((2, C, H, Rc, K), f32),
            V((H, Rc, K), bf16), V((H, Rc, K), bf16),
            V((nK, N, N), bf16), V((nK, N, N), bf16),
            V((T, N, N), bf16), V((T, N, N), bf16),
            V((3, S, S), f32),
            *[V((S, S), bf16)] * 6,
            V((R, N), f32), V((R, N), f32),
            V((2, C, H, Rc, N), f32), V((C, H - 1, Rc, N), f32),
            V((C, Rc, N), f32), V((C, Rc, N), f32), V((C, Rc, N), f32),
            V((C, T, Rc, N), f32), V((C, T, Rc, N), f32),
            V((C, H, H, Rc, Nh), f32), V((C, H - 1, H, Rc, Nh), f32), V((H, C, Rc, Nh), f32),
            V((C, H, Rc, Nh), f32), V((C, H, Rc, Nh), f32),
            V((H, R, Nh), f32), V((H, R, Nh), f32), V((H, R, Nh), f32),
            V((C, H, Rc, Nh), f32), V((C, H, Rc, Nh), f32),
            V((H, R, Nh), f32), V((H, R, Nh), f32),
            V((H, C, Rc, Nh), bf16), V((H, C, Rc, Nh), bf16),
            *[V((H, R, Nh), bf16)] * 4,
            D((nK,)), D((2, C, H)), D((T,)), D((5,)),
            D((C, H - 1)), D((C, H - 1)), D((3 * C + 2, H - 1)), D((3 * C + 2, H - 1)),
            D((2, C, Z)), D((2, C, Z)), D((2, C, Z)), D((2, C, Z)), D((2, C, Z)),
        ],
        compiler_params=pltpu.CompilerParams(
            collective_id=0, has_side_effects=True, vmem_limit_bytes=63 * 1024 * 1024
        ),
    )(*operands)


def solution(mesh):
    return jax.shard_map(
        shards,
        mesh=mesh,
        in_specs=(
            P("hist", "tcol"),
            P(None, "hist"),
            P(None, "hist"),
            P(),
            P(None, "tcol"),
            P(),
            P(),
            P(None, "tcol"),
            P(None, "tcol"),
        ),
        out_specs=(P("hist", "tcol"), P("hist", "tcol")),
        check_vma=False,
    )
```

```python
import functools

import jax
import jax.numpy as jnp
from jax import lax
from jax.experimental import pallas as pl
from jax.experimental.pallas import tpu as pltpu
from jax.sharding import PartitionSpec as P

strength = 0.2
step_size = 0.5
MESH = pl.DeviceIdType.MESH
f32 = jnp.float32
bf16 = jnp.bfloat16


def cubic_power(value):
    return strength * value * value * value


def halves(value):
    high = value.astype(bf16)
    return high, (value - high.astype(f32)).astype(bf16)


def mm(left, right):
    return jnp.dot(left, right, preferred_element_type=f32)


def kernel(
    H, T, C,
    hist_ref, w1_ref, w2_ref, link_ref, prop_ref, inv1_ref, inv2_ref, e1_ref, e2_ref,
    o1_ref, o2_ref,
    hbuf, wbuf, wh, wl, sh, sl, ph, plo, mat, ih, il, kh, kl, vh, vl, e1, e2,
    part, rs, pred, acc1, acc2, g1, g2, nsend, nrecv, rsend, rf, s1, orecv,
    ysend, yrecv, bsend, brecv, x2, q2, r2, t2,
    hsem, wsem, psem, msem, rs_send, rs_recv, x_sent, x_got,
    sp, sr, sleft, rz, rp,
):
    K, N = hist_ref.shape
    R = w1_ref.shape[1]
    S = R * H
    Rc = R // C
    Nh = N // H
    nK = K // N
    Z = T // 2
    h = lax.axis_index("hist")
    t = lax.axis_index("tcol")
    p = t // 2
    core = t % 2
    other = 1 - core
    tile = 32

    def peer(d):
        if H & (H - 1):
            return None
        value, bit = h, 1
        while bit < H:
            if d & bit:
                value = value + bit * (1 - 2 * ((h // bit) % 2))
            bit *= 2
        return value

    order = sorted(range(1, H), key=lambda d: -bin(d).count("1"))

    def split(source, high, low, rows, function=lambda v: v):
        @pl.loop(0, rows // tile)
        def _(i):
            at = pl.ds(pl.multiple_of(i * tile, tile), tile)
            a, b = halves(function(source[at, :]))
            high[at, :] = a
            low[at, :] = b

    def chunk(c, n=1):
        return pl.ds(c * Rc, n * Rc)

    def hist_copy(kb):
        return pltpu.make_async_copy(hist_ref.at[pl.ds(kb * N, N), :], hbuf.at[kb], hsem.at[kb])

    def w_copy(w, c):
        ref = (w1_ref, w2_ref)[w]
        return pltpu.make_async_copy(ref.at[:, chunk(c), :], wbuf.at[w, c], wsem.at[w, c])

    def w_load(w, c):
        w_copy(w, c).start()

    def p_copy(b):
        return pltpu.make_async_copy(
            prop_ref.at[pl.ds(b * N, N), :], hbuf.at[b % nK], psem.at[b % nK]
        )

    own_rows = pl.ds(pl.multiple_of(h * R, R), R)
    small = (
        pltpu.make_async_copy(e1_ref.at[own_rows, :], e1, msem.at[0]),
        pltpu.make_async_copy(inv1_ref, mat.at[0], msem.at[1]),
        pltpu.make_async_copy(link_ref, mat.at[1], msem.at[1]),
        pltpu.make_async_copy(inv2_ref, mat.at[2], msem.at[1]),
        pltpu.make_async_copy(e2_ref.at[own_rows, :], e2, msem.at[2]),
    )

    hist_copy(0).start()
    w_load(0, 0)
    for kb in range(1, nK):
        hist_copy(kb).start()

    barrier = pltpu.get_barrier_semaphore()

    def greet(device):
        pl.semaphore_signal(barrier, inc=1, device_id=device, device_id_type=MESH)

    for d in range(1, H):
        greet({"hist": peer(d)})
    greet({"tcol": p * 2 + other})
    greet({"tcol": lax.rem(p + 1, Z) * 2 + core})
    greet({"tcol": lax.rem(p + Z - 1, Z) * 2 + core})

    def w_split(w, c):
        w_copy(w, c).wait()
        step = 16

        @pl.loop(0, H)
        def _(j):
            for i in range(Rc // step):
                at = pl.ds(i * step, step)
                wh[j, at, :], wl[j, at, :] = halves(wbuf[w, c, j, at, :])

    def w_step(w, c, kb):
        cols = pl.ds(kb * N, N)
        a = wh[:, :, cols].reshape(H * Rc, N)
        b = wl[:, :, cols].reshape(H * Rc, N)
        value = mm(a, sh[kb]) + mm(b, sh[kb]) + mm(a, sl[kb])
        value = value.reshape(H, Rc, N)
        if kb == 0:
            part[w, c] = value
        else:
            part[w, c] += value

    def history_sum(w, c):
        w_split(w, c)
        for kb in range(nK):
            w_step(w, c, kb)

    def rs_copy(c, d):
        return pltpu.make_async_remote_copy(
            src_ref=part.at[0, c, peer(d)], dst_ref=rs.at[c, d - 1],
            send_sem=rs_send, recv_sem=rs_recv.at[c],
            device_id={"hist": peer(d)}, device_id_type=MESH,
        )

    def local_wait(ref, sem):
        pltpu.make_async_copy(ref, ref, sem).wait()

    others = pl.ds(0, H - 1)
    plans = {}
    for c in range(C):
        plans[c] = (
            0, lambda dst, c=c: nsend.at[c, dst], lambda src, d, c=c: nrecv.at[c, d - 1], nrecv.at[c])
        plans[C + c] = (
            1, lambda dst, c=c: rsend.at[c, dst], lambda src, d, c=c: rf.at[c, src], rf.at[c, others])
        plans[2 * C + c] = (
            2, lambda dst, c=c: ysend.at[c, dst], lambda src, d, c=c: yrecv.at[c, src], yrecv.at[c, others])
    plans[3 * C] = (3, lambda dst: s1.at[dst], lambda src, d: orecv.at[src], orecv.at[others])
    plans[3 * C + 1] = (4, lambda dst: bsend.at[dst], lambda src, d: brecv.at[src], brecv.at[others])
    sent = (nsend.at[:, others], rsend.at[:, others], ysend.at[:, others], s1.at[others], bsend.at[others])

    def x_start(kind):
        group, source, target, _ = plans[kind]
        for d in order:
            pltpu.make_async_remote_copy(
                src_ref=source(peer(d)), dst_ref=target(h, d),
                send_sem=x_sent.at[group], recv_sem=x_got.at[kind],
                device_id={"hist": peer(d)}, device_id_type=MESH,
            ).start()

    def x_wait(kind):
        local_wait(plans[kind][3], x_got.at[kind])

    def x_sent_wait(group):
        local_wait(sent[group], x_sent.at[group])

    def z_copy(g, st, c, q, where):
        block = g.at[2 * q + core, chunk(c), :]
        send, recv, target = {
            "partner": (sp, rp, p * 2 + other),
            "right": (sr, rz, t + 2),
            "left": (sleft, rz, t - 2),
        }[where]
        return pltpu.make_async_remote_copy(
            src_ref=block, dst_ref=block,
            send_sem=send.at[st], recv_sem=recv.at[st, c, q],
            device_id={"tcol": target}, device_id_type=MESH,
        )

    def z_partner_wait(g, st, c, q):
        local_wait(g.at[2 * q + other, chunk(c), :], rp.at[st, c, q])

    def z_own(g, st, c):
        @pl.when(p + 1 < Z)
        def _():
            z_copy(g, st, c, p, "right").start()

        @pl.when(p > 0)
        def _():
            z_copy(g, st, c, p, "left").start()

        z_copy(g, st, c, p, "partner").start()

    def z_forward(g, st, c, s):
        @pl.when(p >= s)
        def _():
            q = p - s
            local_wait(g.at[2 * q + core, chunk(c), :], rz.at[st, c, q])

            @pl.when(p + 1 < Z)
            def _():
                z_copy(g, st, c, q, "right").start()

            z_copy(g, st, c, q, "partner").start()

        @pl.when(p + s < Z)
        def _():
            q = p + s
            local_wait(g.at[2 * q + core, chunk(c), :], rz.at[st, c, q])

            @pl.when(p > 0)
            def _():
                z_copy(g, st, c, q, "left").start()

            z_copy(g, st, c, q, "partner").start()

    def z_finish(g, st):
        local_wait(g.at[pl.ds(0, Z)], sp.at[st])
        for k in range(Z):
            if k + 1 < Z:
                @pl.when(p == k)
                def _():
                    local_wait(g.at[pl.ds(0, k + 1)], sr.at[st])
            if k > 0:
                @pl.when(p == k)
                def _():
                    local_wait(g.at[pl.ds(0, Z - k)], sleft.at[st])

    def chip_product(g, acc, q, c, n, first=False):
        at = chunk(c, n)
        m = n * Rc
        left = jnp.concatenate([g[2 * q, at, :], g[2 * q + 1, at, :]], axis=1)
        high, low = halves(left)
        both = mm(jnp.concatenate([high, low], axis=0), ph[pl.ds(2 * q, 2)].reshape(2 * N, N))
        value = both[:m] + both[m:] + mm(high, plo[pl.ds(2 * q, 2)].reshape(2 * N, N))
        if first:
            acc[at, :] = value
        else:
            acc[at, :] += value

    def use_own(g, st, acc, c, n):
        for k in range(c, c + n):
            z_partner_wait(g, st, k, p)
        chip_product(g, acc, p, c, n, True)

    def use(g, st, acc, s, c, n):
        @pl.when(p >= s)
        def _():
            for k in range(c, c + n):
                z_partner_wait(g, st, k, p - s)
            chip_product(g, acc, p - s, c, n)

        @pl.when(p + s < Z)
        def _():
            for k in range(c, c + n):
                z_partner_wait(g, st, k, p + s)
            chip_product(g, acc, p + s, c, n)

    last = max(Z, 2)

    def gather(g, st, acc, begin, after, done, first_round=0):
        for r in range(first_round, C + last + 1):
            if begin and r < C:
                begin(r)
            for s in range(1, Z):
                if 0 <= r - s < C:
                    z_forward(g, st, r - s, s)
            for s in range(Z):
                c = r - 1 - max(s, 0)
                if s == Z - 1 and Z > 1:
                    if 0 <= c < C:
                        use(g, st, acc, s, c, 1)
                elif 1 <= c < C and c % 2 == 1:
                    if s == 0:
                        use_own(g, st, acc, c - 1, 2)
                    else:
                        use(g, st, acc, s, c - 1, 2)
            if 0 <= r - last < C:
                done(r - last)
            if r in after:
                after[r]()

    w_split(0, 0)
    for kb in range(nK):
        hist_copy(kb).wait()
        split(hbuf.at[kb], sh.at[kb], sl.at[kb], N, cubic_power)
        w_step(0, 0, kb)
        if kb + 1 < C:
            w_load(0, kb + 1)
    for c in range(nK + 1, C):
        w_load(0, c)
    pl.semaphore_wait(barrier, H + 2)
    for d in order:
        rs_copy(0, d).start()
    small[0].start()
    w_load(1, 0)
    small[4].start()
    for c in range(1, C):
        history_sum(0, c)
        for d in order:
            rs_copy(c, d).start()
        w_load(1, c)
    for b in range(nK):
        p_copy(b).start()
    for copy in small[1:4]:
        copy.start()
    small[0].wait()
    small[4].wait()

    def begin_one(c):
        local_wait(rs.at[c], rs_recv.at[c])
        total = part[0, c, h] + e1[chunk(c), :]
        for d in range(1, H):
            total += rs[c, d - 1]
        pred[chunk(c), :] = total
        g1[t, chunk(c), :] = cubic_power(total)
        z_own(g1, 0, c)

    def near_sums(c):
        history_sum(1, c)
        part[1, c, h] += e2[chunk(c), :]
        for j in range(H):
            nsend[c, j] = part[1, c, :, :, j * Nh:(j + 1) * Nh]

    def p_split(b):
        p_copy(b).wait()
        split(hbuf.at[b % nK], ph.at[b], plo.at[b], N)
        if b + nK < T:
            p_copy(b + nK).start()

    def split_matrices():
        pltpu.make_async_copy(mat, mat, msem.at[1]).wait()
        split(mat.at[0], ih, il, S)
        split(mat.at[1], kh, kl, S)

        @pl.loop(0, H)
        def _(j):
            for c in range(C):
                at = pl.ds(pl.multiple_of(j * R + c * Rc, Rc), Rc)
                vh[c, j], vl[c, j] = halves(mat[2, at, :])

    def send_right(c):
        value = pred[chunk(c), :] + step_size * acc1[chunk(c), :]
        for j in range(H):
            rsend[c, j] = value[:, j * Nh:(j + 1) * Nh]
        x_start(C + c)
        rf[c, h] = rsend[c, h]

    def near(c):
        near_sums(c)
        x_start(c)

    def after0():
        for b in range(T // 2):
            p_split(b)
        near(1)

    def after1():
        for b in range(T // 2, T):
            p_split(b)
        near(2)

    def after2():
        near(3)

    near(0)
    gather(g1, 0, acc1, begin_one, {0: after0, 1: after1, 2: after2, 4: split_matrices}, send_right)

    def pair_store(ref, at, value):
        a, b = halves(value)
        ref[at, :Nh] = a
        ref[at, Nh:] = b

    for c in range(C):
        x_wait(C + c)
        for j in range(H):
            pair_store(x2, pl.ds(j * R + c * Rc, Rc), rf[c, j])

    def apply(high, low, source):
        wide = mm(high, source[...])
        return wide[:, :Nh] + wide[:, Nh:] + mm(low, source[:, :Nh])

    for j in range(H):
        at = pl.ds(j * R, R)
        value = apply(ih[at, :], il[at, :], x2)
        s1[j] = value
        pair_store(q2, at, cubic_power(value))

    for c in range(C):
        x_wait(c)
    for j in range(H):
        at = pl.ds(j * R, R)
        value = apply(kh[at, :], kl[at, :], q2)
        base = []
        for c in range(C):
            total = nsend[c, h, j]
            for d in range(1, H):
                total += nrecv[c, d - 1, j]
            base.append(total)
        value += jnp.concatenate(base, axis=0)
        pair_store(r2, at, step_size * cubic_power(value))
        pair_store(t2, at, value)

    for c in range(C):
        value = apply(vh[c].reshape(H * Rc, S), vl[c].reshape(H * Rc, S), r2)
        ysend[c] = value.reshape(H, Rc, Nh)
        x_start(2 * C + c)
        yrecv[c, h] = ysend[c, h]
    x_start(3 * C)
    orecv[h] = s1[h]

    for c in range(C):
        value = apply(vh[c].reshape(H * Rc, S), vl[c].reshape(H * Rc, S), t2)
        bsend[:, chunk(c), :] = value.reshape(H, Rc, Nh)

    def begin_two(c):
        x_wait(2 * C + c)
        g2[t, chunk(c), :] = jnp.concatenate([yrecv[c, j] for j in range(H)], axis=1)
        z_own(g2, 1, c)

    for c in range(C):
        begin_two(c)
    x_start(3 * C + 1)
    brecv[h] = bsend[h]

    def drain_one():
        local_wait(part.at[0, :, others], rs_send)
        z_finish(g1, 0)
        x_sent_wait(0)
        x_sent_wait(1)

    def drain_two():
        x_wait(3 * C)
        for j in range(H):
            o1_ref[:, j * Nh:(j + 1) * Nh] = orecv[j]
        x_wait(3 * C + 1)
        for group in (2, 3, 4):
            x_sent_wait(group)

    drain_one()

    def finish(c):
        at = chunk(c)
        o2_ref[at, :] = acc2[at, :] + jnp.concatenate([brecv[j, at, :] for j in range(H)], axis=1)

    gather(g2, 1, acc2, None, {3: drain_two}, finish, 1)
    z_finish(g2, 1)


def shards(*operands):
    history, w1, w2 = operands[:3]
    K, N = history.shape
    S = w1.shape[0]
    H, T, C = lax.axis_size("hist"), lax.axis_size("tcol"), 4
    R = S // H
    Rc, Nh, nK, Z = R // C, N // H, K // N, T // 2
    split_rows = lambda w: w.reshape(H, R, K)
    V, D = pltpu.VMEM, pltpu.SemaphoreType.DMA
    return pl.pallas_call(
        functools.partial(kernel, H, T, C),
        out_shape=[pltpu.VMEM((R, N), f32)] * 2,
        in_specs=[pl.BlockSpec(memory_space=pl.ANY)] * 9,
        out_specs=[pl.BlockSpec(memory_space=pltpu.VMEM)] * 2,
        scratch_shapes=[
            V((nK, N, N), f32), V((2, C, H, Rc, K), f32),
            V((H, Rc, K), bf16), V((H, Rc, K), bf16),
            V((nK, N, N), bf16), V((nK, N, N), bf16),
            V((T, N, N), bf16), V((T, N, N), bf16),
            V((3, S, S), f32),
            *[V((S, S), bf16)] * 4, *[V((C, H, Rc, S), bf16)] * 2,
            V((R, N), f32), V((R, N), f32),
            V((2, C, H, Rc, N), f32), V((C, H - 1, Rc, N), f32),
            V((R, N), f32), V((R, N), f32), V((R, N), f32),
            V((T, R, N), f32), V((T, R, N), f32),
            V((C, H, H, Rc, Nh), f32), V((C, H - 1, H, Rc, Nh), f32),
            V((C, H, Rc, Nh), f32), V((C, H, Rc, Nh), f32),
            V((H, R, Nh), f32), V((H, R, Nh), f32),
            V((C, H, Rc, Nh), f32), V((C, H, Rc, Nh), f32),
            V((H, R, Nh), f32), V((H, R, Nh), f32),
            *[V((S, 2 * Nh), bf16)] * 4,
            D((nK,)), D((2, C)), D((nK,)), D((3,)),
            D, D((C,)), D((5,)), D((3 * C + 2,)),
            D((2,)), D((2,)), D((2,)), D((2, C, Z)), D((2, C, Z)),
        ],
        compiler_params=pltpu.CompilerParams(
            collective_id=0, has_side_effects=True, vmem_limit_bytes=63 * 1024 * 1024
        ),
    )(history, split_rows(w1), split_rows(w2), *operands[3:])


def solution(mesh):
    return jax.shard_map(
        shards,
        mesh=mesh,
        in_specs=(
            P("hist", "tcol"),
            P(None, "hist"),
            P(None, "hist"),
            P(),
            P(None, "tcol"),
            P(),
            P(),
            P(None, "tcol"),
            P(None, "tcol"),
        ),
        out_specs=(P("hist", "tcol"), P("hist", "tcol")),
        check_vma=False,
    )
```

```python
import functools

import jax
import jax.numpy as jnp
from jax import lax
from jax.experimental import pallas as pl
from jax.experimental.pallas import tpu as pltpu
from jax.sharding import PartitionSpec as P

strength = 0.2
step_size = 0.5
MESH = pl.DeviceIdType.MESH
f32 = jnp.float32
bf16 = jnp.bfloat16


def cubic_power(value):
    return strength * value * value * value


def halves(value):
    high = value.astype(bf16)
    return high, (value - high.astype(f32)).astype(bf16)


def mm(left, right):
    return jnp.dot(left, right, preferred_element_type=f32)


def kernel(
    H, T, C,
    hist_ref, w1_ref, w2_ref, link_ref, prop_ref, inv1_ref, inv2_ref, e1_ref, e2_ref,
    o1_ref, o2_ref,
    hbuf, wbuf, wh, wl, sh, sl, ph, plo, mat, ih, il, kh, kl, vh, vl, e1, e2,
    part, rs, pred, acc1, acc2, g1, g2, nsend, nmid, nrecv, rsend, rf, s1, orecv,
    ysend, yrecv, bsend, brecv, x2, q2, r2, t2,
    hsem, wsem, psem, msem, rs_send, rs_recv, x_sent, x_got,
    sp, sin, sout, rz, rp,
):
    K, N = hist_ref.shape
    R = w1_ref.shape[1]
    S = R * H
    Rc = R // C
    Nh = N // H
    nK = K // N
    Z = T // 2
    h = lax.axis_index("hist")
    t = lax.axis_index("tcol")
    p = t // 2
    core = t % 2
    other = 1 - core
    half = (Z + 1) // 2
    upper = p // half
    inward = 1 - 2 * upper
    rim = p + upper * (Z - 1 - 2 * p)
    tile = 32

    def peer(d):
        if H & (H - 1):
            return None
        value, bit = h, 1
        while bit < H:
            if d & bit:
                value = value + bit * (1 - 2 * ((h // bit) % 2))
            bit *= 2
        return value

    order = sorted(range(1, H), key=lambda d: -bin(d).count("1"))

    def split(source, high, low, rows, function=lambda v: v, unroll=1):
        @pl.loop(0, rows // tile, unroll=unroll)
        def _(i):
            at = pl.ds(pl.multiple_of(i * tile, tile), tile)
            a, b = halves(function(source[at, :]))
            high[at, :] = a
            low[at, :] = b

    def chunk(c, n=1):
        return pl.ds(c * Rc, n * Rc)

    def hist_copy(kb):
        return pltpu.make_async_copy(hist_ref.at[pl.ds(kb * N, N), :], hbuf.at[kb], hsem.at[kb])

    def w_copy(w, c):
        ref = (w1_ref, w2_ref)[w]
        return pltpu.make_async_copy(ref.at[:, chunk(c), :], wbuf.at[w, c], wsem.at[w, c])

    def w_load(w, c):
        w_copy(w, c).start()

    def p_copy(b):
        return pltpu.make_async_copy(
            prop_ref.at[pl.ds(b * N, N), :], hbuf.at[b % nK], psem.at[b % nK]
        )

    own_rows = pl.ds(pl.multiple_of(h * R, R), R)
    small = (
        pltpu.make_async_copy(e1_ref.at[own_rows, :], e1, msem.at[0]),
        pltpu.make_async_copy(inv1_ref, mat.at[0], msem.at[1]),
        pltpu.make_async_copy(link_ref, mat.at[1], msem.at[1]),
        pltpu.make_async_copy(inv2_ref, mat.at[2], msem.at[1]),
        pltpu.make_async_copy(e2_ref.at[own_rows, :], e2, msem.at[2]),
    )

    hist_copy(0).start()
    w_load(0, 0)
    for kb in range(1, nK):
        hist_copy(kb).start()

    barrier = pltpu.get_barrier_semaphore()

    def greet(device):
        pl.semaphore_signal(barrier, inc=1, device_id=device, device_id_type=MESH)

    for d in range(1, H):
        greet({"hist": peer(d)})
    greet({"tcol": p * 2 + other})
    greet({"tcol": lax.rem(p + 1, Z) * 2 + core})
    greet({"tcol": lax.rem(p + Z - 1, Z) * 2 + core})

    def w_split(w, c):
        w_copy(w, c).wait()
        step = 16

        @pl.loop(0, H)
        def _(j):
            for i in range(Rc // step):
                at = pl.ds(i * step, step)
                wh[j, at, :], wl[j, at, :] = halves(wbuf[w, c, j, at, :])

    def w_step(w, c, kb):
        cols = pl.ds(kb * N, N)
        a = wh[:, :, cols].reshape(H * Rc, N)
        b = wl[:, :, cols].reshape(H * Rc, N)
        value = mm(a, sh[kb]) + mm(b, sh[kb]) + mm(a, sl[kb])
        value = value.reshape(H, Rc, N)
        if kb == 0:
            part[w, c] = value
        else:
            part[w, c] += value

    def history_sum(w, c):
        w_split(w, c)
        for kb in range(nK):
            w_step(w, c, kb)

    def rs_copy(c, d):
        return pltpu.make_async_remote_copy(
            src_ref=part.at[0, c, peer(d)], dst_ref=rs.at[c, d - 1],
            send_sem=rs_send, recv_sem=rs_recv.at[c],
            device_id={"hist": peer(d)}, device_id_type=MESH,
        )

    def local_wait(ref, sem):
        pltpu.make_async_copy(ref, ref, sem).wait()

    others = pl.ds(0, H - 1)
    plans = {}
    for c in range(C):
        plans[C + c] = (
            1, lambda dst, c=c: rsend.at[c, dst], lambda src, d, c=c: rf.at[c, src], rf.at[c, others])
        plans[2 * C + c] = (
            2, lambda dst, c=c: ysend.at[c, dst], lambda src, d, c=c: yrecv.at[c, src], yrecv.at[c, others])
    plans[3 * C] = (3, lambda dst: s1.at[dst], lambda src, d: orecv.at[src], orecv.at[others])
    plans[3 * C + 1] = (4, lambda dst: bsend.at[dst], lambda src, d: brecv.at[src], brecv.at[others])
    sent = (nsend.at[:, others], rsend.at[:, others], ysend.at[:, others], s1.at[others], bsend.at[others])

    def x_start(kind):
        group, source, target, _ = plans[kind]
        for d in order:
            pltpu.make_async_remote_copy(
                src_ref=source(peer(d)), dst_ref=target(h, d),
                send_sem=x_sent.at[group], recv_sem=x_got.at[kind],
                device_id={"hist": peer(d)}, device_id_type=MESH,
            ).start()

    def x_wait(kind):
        local_wait(plans[kind][3], x_got.at[kind])

    def near_plan(c):
        bit = 1 if c % 2 == 0 else max(H // 2, 1)
        return bit, [e for e in range(H) if not e & bit]

    def near_copy(c, to, block, target, sem):
        pltpu.make_async_remote_copy(
            src_ref=nsend.at[c, peer(block)], dst_ref=target,
            send_sem=x_sent.at[0], recv_sem=sem,
            device_id={"hist": peer(to)}, device_id_type=MESH,
        ).start()

    def near_start(c):
        bit, rest = near_plan(c)
        for i, e in enumerate(rest):
            near_copy(c, bit, bit | e, nmid.at[c, i], x_got.at[c])

    def near_middle(c):
        bit, rest = near_plan(c)
        local_wait(nmid.at[c], x_got.at[c])
        for i, e in enumerate(rest):
            nsend[c, peer(e)] += nmid[c, i]
        for i, e in enumerate(rest[1:]):
            near_copy(c, e, e, nrecv.at[c, i], x_got.at[3 * C + 2 + c])

    def x_sent_wait(group):
        local_wait(sent[group], x_sent.at[group])

    def z_copy(g, st, c, q, where):
        block = g.at[2 * q + core, chunk(c), :]
        send, recv, target = {
            "partner": (sp, rp, p * 2 + other),
            "in": (sin, rz, t + 2 * inward),
            "out": (sout, rz, t - 2 * inward),
        }[where]
        return pltpu.make_async_remote_copy(
            src_ref=block, dst_ref=block,
            send_sem=send.at[st], recv_sem=recv.at[st, c // 2 if where == "partner" else c, q],
            device_id={"tcol": target}, device_id_type=MESH,
        )

    def z_partner_wait(g, st, c, q):
        local_wait(g.at[2 * q + other, chunk(c, 2), :], rp.at[st, c // 2, q])

    def z_own(g, st, c):
        @pl.when(rim > 0)
        def _():
            z_copy(g, st, c, p, "out").start()

        if Z > 1:
            @pl.when(rim < Z - 1)
            def _():
                z_copy(g, st, c, p, "in").start()

        z_copy(g, st, c, p, "partner").start()

    def exists(side, s):
        return rim < Z - s if side == "in" else rim >= s

    def place(side, s):
        return p + s * inward if side == "in" else p - s * inward

    def z_forward(g, st, side, s, c):
        if s >= (Z if side == "in" else half):
            return

        @pl.when(exists(side, s))
        def _():
            q = place(side, s)
            local_wait(g.at[2 * q + core, chunk(c), :], rz.at[st, c, q])
            if side == "in":
                @pl.when(rim > 0)
                def _():
                    z_copy(g, st, c, q, "out").start()
            else:
                z_copy(g, st, c, q, "in").start()
            z_copy(g, st, c, q, "partner").start()

    def z_finish(g, st):
        local_wait(g.at[pl.ds(0, Z)], sp.at[st])
        for k in range(half):
            @pl.when(rim == k)
            def _():
                if k + 1 < Z:
                    local_wait(g.at[pl.ds(0, k + 1)], sin.at[st])
                if k > 0:
                    local_wait(g.at[pl.ds(0, Z - k)], sout.at[st])

    def chip_product(g, acc, q, c, n, first=False):
        at = chunk(c, n)
        m = n * Rc
        left = jnp.concatenate([g[2 * q, at, :], g[2 * q + 1, at, :]], axis=1)
        high, low = halves(left)
        both = mm(jnp.concatenate([high, low], axis=0), ph[pl.ds(2 * q, 2)].reshape(2 * N, N))
        value = both[:m] + both[m:] + mm(high, plo[pl.ds(2 * q, 2)].reshape(2 * N, N))
        if first:
            acc[at, :] = value
        else:
            acc[at, :] += value

    def use_own(g, st, acc, c, n):
        for k in range(c, c + n, 2):
            z_partner_wait(g, st, k, p)
        chip_product(g, acc, p, c, n, True)

    def use(g, st, acc, side, s, c, n):
        if s >= (Z if side == "in" else half):
            return

        @pl.when(exists(side, s))
        def _():
            q = place(side, s)
            for k in range(c, c + n, 2):
                z_partner_wait(g, st, k, q)
            chip_product(g, acc, q, c, n)

    def near(c):
        near_sums(c)
        near_start(c)

    def p_half(k):
        for b in range(k * (T // 2), (k + 1) * (T // 2)):
            p_split(b)

    def gather(g, st, acc, steps, actions):
        for step in steps:
            name = step[0]
            if name in ("in", "out"):
                z_forward(g, st, name, step[1], step[2])
            elif name == "own":
                use_own(g, st, acc, *step[1:])
            elif name == "use":
                use(g, st, acc, *step[1:])
            else:
                actions[name](*step[1:])

    def one_steps():
        deep = range(3, Z)
        yield ("near", 0)
        yield ("begin", 0)
        yield ("near", 1)
        yield ("near", 2)
        yield ("begin", 1)
        yield ("split", 0)
        yield ("in", 1, 0)
        yield ("out", 1, 0)
        yield ("near", 3)
        yield ("begin", 2)
        yield ("split", 1)
        yield ("in", 1, 1)
        yield ("out", 1, 1)
        yield ("in", 2, 0)
        yield ("own", 0, 2)
        yield ("begin", 3)
        yield ("use", "in", 1, 0, 2)
        yield ("in", 1, 2)
        yield ("out", 1, 2)
        yield ("use", "out", 1, 0, 2)
        yield ("in", 2, 1)
        for s in deep:
            yield ("in", s, 0)
        yield ("middle", 0)
        yield ("middle", 1)
        yield ("matrices",)
        yield ("in", 1, 3)
        yield ("out", 1, 3)
        yield ("use", "in", 2, 0, 2)
        yield ("early", 0)
        yield ("early", 1)
        yield ("own", 2, 2)
        for s in range(2, half):
            for c in range(C):
                yield ("out", s, c)
            yield ("use", "out", s, 0, C)
        yield ("in", 2, 2)
        yield ("middle", 2)
        yield ("middle", 3)
        for s in deep:
            yield ("in", s, 1)
        yield ("use", "in", 1, 2, 2)
        yield ("use", "out", 1, 2, 2)
        for s in deep:
            yield ("use", "in", s, 0, 2)
        yield ("late", 0)
        yield ("late", 1)
        yield ("in", 2, 3)
        for s in deep:
            yield ("in", s, 2)
        yield ("use", "in", 2, 2, 2)
        for s in deep:
            yield ("in", s, 3)
        for s in deep:
            yield ("use", "in", s, 2, 2)
        yield ("done", 2)
        yield ("done", 3)

    def two_steps():
        for c in range(C):
            yield ("begin", c)
        yield ("rest",)
        yield ("drain", 0)
        yield ("own", 0, C)
        for c in range(C):
            yield ("in", 1, c)
        yield ("out", 1, 0)
        yield ("out", 1, 1)
        yield ("use", "in", 1, 0, C)
        yield ("out", 1, 2)
        yield ("in", 2, 0)
        yield ("out", 1, 3)
        yield ("in", 2, 1)
        for s in range(2, half):
            for c in range(C):
                yield ("out", s, c)
            yield ("use", "out", s, 0, C)
        yield ("in", 2, 2)
        yield ("in", 2, 3)
        yield ("drain", 1)
        yield ("use", "out", 1, 0, C)
        for s in range(3, Z):
            yield ("in", s, 0)
            yield ("in", s, 1)
        for s in range(2, Z):
            yield ("use", "in", s, 0, 2)
        yield ("done", 0)
        yield ("done", 1)
        yield ("use", "in", 2, 2, 2)
        for s in range(3, Z):
            yield ("in", s, 2)
            yield ("in", s, 3)
            yield ("use", "in", s, 2, 2)
        yield ("done", 2)
        yield ("done", 3)

    w_split(0, 0)
    for kb in range(nK):
        hist_copy(kb).wait()
        split(hbuf.at[kb], sh.at[kb], sl.at[kb], N, cubic_power, 4)
        w_step(0, 0, kb)
        if kb + 1 < C:
            w_load(0, kb + 1)
    for c in range(nK + 1, C):
        w_load(0, c)
    pl.semaphore_wait(barrier, H + 2)
    for d in order:
        rs_copy(0, d).start()
    small[0].start()
    w_load(1, 0)
    small[4].start()
    for c in range(1, C):
        history_sum(0, c)
        for d in order:
            rs_copy(c, d).start()
        w_load(1, c)
    for b in range(nK):
        p_copy(b).start()
    for copy in small[1:4]:
        copy.start()
    small[0].wait()
    small[4].wait()

    def begin_one(c):
        local_wait(rs.at[c], rs_recv.at[c])
        total = part[0, c, h] + e1[chunk(c), :]
        for d in range(1, H):
            total += rs[c, d - 1]
        pred[chunk(c), :] = total
        g1[t, chunk(c), :] = cubic_power(total)
        z_own(g1, 0, c)

    def near_sums(c):
        history_sum(1, c)
        part[1, c, h] += e2[chunk(c), :]
        for j in range(H):
            nsend[c, j] = part[1, c, :, :, j * Nh:(j + 1) * Nh]

    def p_split(b):
        p_copy(b).wait()
        split(hbuf.at[b % nK], ph.at[b], plo.at[b], N)
        if b + nK < T:
            p_copy(b + nK).start()

    def split_matrices():
        pltpu.make_async_copy(mat, mat, msem.at[1]).wait()
        split(mat.at[0], ih, il, S)
        split(mat.at[1], kh, kl, S)

        @pl.loop(0, H)
        def _(j):
            for c in range(C):
                at = pl.ds(pl.multiple_of(j * R + c * Rc, Rc), Rc)
                vh[c, j], vl[c, j] = halves(mat[2, at, :])

    def send_right(c):
        value = pred[chunk(c), :] + step_size * acc1[chunk(c), :]
        for j in range(H):
            rsend[c, j] = value[:, j * Nh:(j + 1) * Nh]
        x_start(C + c)
        rf[c, h] = rsend[c, h]

    ahead = rim >= 1 if Z <= 4 else rim >= Z

    def early(c):
        @pl.when(ahead)
        def _():
            send_right(c)

    def late(c):
        @pl.when(jnp.logical_not(ahead))
        def _():
            send_right(c)

    gather(g1, 0, acc1, one_steps(), {
        "near": near, "middle": near_middle, "early": early, "late": late, "begin": begin_one, "split": p_half, "matrices": split_matrices, "done": send_right,
    })

    def pair_store(ref, at, value):
        a, b = halves(value)
        ref[at, :Nh] = a
        ref[at, Nh:] = b

    for c in range(C):
        x_wait(C + c)
        for j in range(H):
            pair_store(x2, pl.ds(j * R + c * Rc, Rc), rf[c, j])

    def apply(high, low, source):
        wide = mm(high, source[...])
        return wide[:, :Nh] + wide[:, Nh:] + mm(low, source[:, :Nh])

    value = apply(ih[...], il[...], x2)
    s1[...] = value.reshape(H, R, Nh)
    pair_store(q2, pl.ds(0, S), cubic_power(value))

    for c in range(C):
        if H > 2:
            local_wait(nrecv.at[c], x_got.at[3 * C + 2 + c])
    value = apply(kh[...], kl[...], q2)
    base = []
    for j in range(H):
        for c in range(C):
            total = nsend[c, h, j]
            if H > 2:
                for i in range(H // 2 - 1):
                    total += nrecv[c, i, j]
            base.append(total)
    value += jnp.concatenate(base, axis=0)
    pair_store(r2, pl.ds(0, S), step_size * cubic_power(value))
    pair_store(t2, pl.ds(0, S), value)

    for c in range(C):
        value = apply(vh[c].reshape(H * Rc, S), vl[c].reshape(H * Rc, S), r2)
        ysend[c] = value.reshape(H, Rc, Nh)
        x_start(2 * C + c)
        yrecv[c, h] = ysend[c, h]
    for c in range(C):
        value = apply(vh[c].reshape(H * Rc, S), vl[c].reshape(H * Rc, S), t2)
        bsend[:, chunk(c), :] = value.reshape(H, Rc, Nh)

    def begin_two(c):
        x_wait(2 * C + c)
        g2[t, chunk(c), :] = jnp.concatenate([yrecv[c, j] for j in range(H)], axis=1)
        z_own(g2, 1, c)

    def rest():
        x_start(3 * C)
        orecv[h] = s1[h]
        x_start(3 * C + 1)
        brecv[h] = bsend[h]

    def drain_one():
        local_wait(part.at[0, :, others], rs_send)
        z_finish(g1, 0)
        x_sent_wait(0)
        x_sent_wait(1)

    def drain_two():
        x_wait(3 * C)
        for j in range(H):
            o1_ref[:, j * Nh:(j + 1) * Nh] = orecv[j]
        x_wait(3 * C + 1)
        for group in (2, 3, 4):
            x_sent_wait(group)

    def finish(c):
        at = chunk(c)
        o2_ref[at, :] = acc2[at, :] + jnp.concatenate([brecv[j, at, :] for j in range(H)], axis=1)

    gather(g2, 1, acc2, two_steps(), {
        "begin": begin_two, "rest": rest, "drain": lambda k: (drain_one, drain_two)[k](), "done": finish,
    })
    z_finish(g2, 1)


def shards(*operands):
    history, w1, w2 = operands[:3]
    K, N = history.shape
    S = w1.shape[0]
    H, T, C = lax.axis_size("hist"), lax.axis_size("tcol"), 4
    R = S // H
    Rc, Nh, nK, Z = R // C, N // H, K // N, T // 2
    split_rows = lambda w: w.reshape(H, R, K)
    V, D = pltpu.VMEM, pltpu.SemaphoreType.DMA
    return pl.pallas_call(
        functools.partial(kernel, H, T, C),
        out_shape=[pltpu.VMEM((R, N), f32)] * 2,
        in_specs=[pl.BlockSpec(memory_space=pl.ANY)] * 9,
        out_specs=[pl.BlockSpec(memory_space=pltpu.VMEM)] * 2,
        scratch_shapes=[
            V((nK, N, N), f32), V((2, C, H, Rc, K), f32),
            V((H, Rc, K), bf16), V((H, Rc, K), bf16),
            V((nK, N, N), bf16), V((nK, N, N), bf16),
            V((T, N, N), bf16), V((T, N, N), bf16),
            V((3, S, S), f32),
            *[V((S, S), bf16)] * 4, *[V((C, H, Rc, S), bf16)] * 2,
            V((R, N), f32), V((R, N), f32),
            V((2, C, H, Rc, N), f32), V((C, H - 1, Rc, N), f32),
            V((R, N), f32), V((R, N), f32), V((R, N), f32),
            V((T, R, N), f32), V((T, R, N), f32),
            V((C, H, H, Rc, Nh), f32), V((C, H // 2, H, Rc, Nh), f32), V((C, max(H // 2 - 1, 1), H, Rc, Nh), f32),
            V((C, H, Rc, Nh), f32), V((C, H, Rc, Nh), f32),
            V((H, R, Nh), f32), V((H, R, Nh), f32),
            V((C, H, Rc, Nh), f32), V((C, H, Rc, Nh), f32),
            V((H, R, Nh), f32), V((H, R, Nh), f32),
            *[V((S, 2 * Nh), bf16)] * 4,
            D((nK,)), D((2, C)), D((nK,)), D((3,)),
            D, D((C,)), D((5,)), D((4 * C + 2,)),
            D((2,)), D((2,)), D((2,)), D((2, C, Z)), D((2, C // 2, Z)),
        ],
        compiler_params=pltpu.CompilerParams(
            collective_id=0, has_side_effects=True, vmem_limit_bytes=63 * 1024 * 1024
        ),
    )(history, split_rows(w1), split_rows(w2), *operands[3:])


def solution(mesh):
    return jax.shard_map(
        shards,
        mesh=mesh,
        in_specs=(
            P("hist", "tcol"),
            P(None, "hist"),
            P(None, "hist"),
            P(),
            P(None, "tcol"),
            P(),
            P(),
            P(None, "tcol"),
            P(None, "tcol"),
        ),
        out_specs=(P("hist", "tcol"), P("hist", "tcol")),
        check_vma=False,
    )
```

```python
import functools

import jax
import jax.numpy as jnp
from jax import lax
from jax.experimental import pallas as pl
from jax.experimental.pallas import tpu as pltpu
from jax.sharding import PartitionSpec as P

strength = 0.2
step_size = 0.5
MESH = pl.DeviceIdType.MESH
f32 = jnp.float32
bf16 = jnp.bfloat16


def cubic_power(value):
    return strength * value * value * value


def halves(value):
    high = value.astype(bf16)
    return high, (value - high.astype(f32)).astype(bf16)


def mm(left, right):
    return jnp.dot(left, right, preferred_element_type=f32)


def kernel(
    H, T, C,
    hist_ref, w1_ref, w2_ref, link_ref, prop_ref, inv1_ref, inv2_ref, e1_ref, e2_ref,
    o1_ref, o2_ref, zero_ref,
    hbuf, wbuf, wh, wl, sh, sl, ph, plo, mat, ih, il, kh, kl, vh, vl, e1, e2,
    part, rs, pred, acc1, acc2, g1, g2, nsend, nmid, nrecv, rsend, rf, s1, orecv,
    ysend, yrecv, bsend, brecv, x2, q2, r2, t2,
    hsem, wsem, msem, rs_send, rs_recv, x_sent, x_got,
    sp, sin, sout, rz, rp,
):
    K, N = hist_ref.shape
    R = w1_ref.shape[1]
    S = R * H
    Rc = R // C
    F = 2
    Rf = Rc // F
    Nh = N // H
    nK = K // N
    Z = T // 2
    h = lax.axis_index("hist")
    t = lax.axis_index("tcol")
    p = t // 2
    core = t % 2
    other = 1 - core
    half = (Z + 1) // 2
    upper = p // half
    inward = 1 - 2 * upper
    rim = p + upper * (Z - 1 - 2 * p)
    tile = 32

    def peer(d):
        if H & (H - 1):
            return None
        value, bit = h, 1
        while bit < H:
            if d & bit:
                value = value + bit * (1 - 2 * ((h // bit) % 2))
            bit *= 2
        return value

    order = sorted(range(1, H), key=lambda d: -bin(d).count("1"))

    def split(source, high, low, rows, function=lambda v: v, unroll=1):
        @pl.loop(0, rows // tile, unroll=unroll)
        def _(i):
            at = pl.ds(pl.multiple_of(i * tile, tile), tile)
            a, b = halves(function(source[at, :]))
            high[at, :] = a
            low[at, :] = b

    def chunk(c, n=1):
        return pl.ds(c * Rc, n * Rc)

    def fine(f):
        return pl.ds(f * Rf, Rf)

    def inner(f):
        return pl.ds(f % F * Rf, Rf)

    def hist_copy(kb):
        return pltpu.make_async_copy(hist_ref.at[pl.ds(kb * N, N), :], hbuf.at[kb], hsem.at[kb])

    def w_copy(w, c):
        ref = (w1_ref, w2_ref)[w]
        return pltpu.make_async_copy(ref.at[:, chunk(c), :], wbuf.at[w, c], wsem.at[c])

    def w_load(w, c):
        w_copy(w, c).start()

    def p_copy(b):
        return pltpu.make_async_copy(
            prop_ref.at[pl.ds(b * N, N), :], hbuf.at[b % nK], hsem.at[b % nK]
        )

    own_rows = pl.ds(pl.multiple_of(h * R, R), R)
    small = (
        pltpu.make_async_copy(e1_ref.at[own_rows, :], e1, msem.at[0]),
        pltpu.make_async_copy(inv1_ref, mat.at[0], msem.at[1]),
        pltpu.make_async_copy(link_ref, mat.at[1], msem.at[1]),
        pltpu.make_async_copy(inv2_ref, mat.at[2], msem.at[1]),
        pltpu.make_async_copy(e2_ref.at[own_rows, :], e2, msem.at[2]),
    )

    hist_copy(0).start()
    w_load(0, 0)
    for kb in range(1, nK):
        hist_copy(kb).start()

    barrier = pltpu.get_barrier_semaphore()

    def greet(device):
        pl.semaphore_signal(barrier, inc=1, device_id=device, device_id_type=MESH)

    for d in range(1, H):
        greet({"hist": peer(d)})
    greet({"tcol": p * 2 + other})
    greet({"tcol": lax.rem(p + 1, Z) * 2 + core})
    greet({"tcol": lax.rem(p + Z - 1, Z) * 2 + core})

    def w_split(w, c):
        w_copy(w, c).wait()
        step = 16

        @pl.loop(0, H)
        def _(j):
            for i in range(Rc // step):
                at = pl.ds(i * step, step)
                wh[j, at, :], wl[j, at, :] = halves(wbuf[w, c, j, at, :])

    def w_step(w, c, kb):
        cols = pl.ds(kb * N, N)
        a = wh[:, :, cols].reshape(H * Rc, N)
        b = wl[:, :, cols].reshape(H * Rc, N)
        value = mm(a, sh[kb]) + mm(b, sh[kb]) + mm(a, sl[kb])
        value = value.reshape(H, Rc, N)
        if kb == 0:
            part[w, c] = value
        else:
            part[w, c] += value

    def history_sum(w, c):
        w_split(w, c)
        for kb in range(nK):
            w_step(w, c, kb)

    def rs_copy(f, d):
        return pltpu.make_async_remote_copy(
            src_ref=part.at[0, f // F, peer(d), inner(f), :], dst_ref=rs.at[f // F, d - 1, inner(f), :],
            send_sem=rs_send, recv_sem=rs_recv.at[f],
            device_id={"hist": peer(d)}, device_id_type=MESH,
        )

    def rs_start(c):
        for f in range(c * F, c * F + F):
            for d in order:
                rs_copy(f, d).start()

    def local_wait(ref, sem):
        pltpu.make_async_copy(ref, ref, sem).wait()

    others = pl.ds(0, H - 1)
    plans = {}
    for c in range(C):
        plans[C + c] = (
            1, lambda dst, c=c: rsend.at[c, dst], lambda src, d, c=c: rf.at[c, src], rf.at[c, others], x_got.at[C + c])
        plans[2 * C + c] = (
            2, lambda dst, c=c: ysend.at[c, dst], lambda src, d, c=c: yrecv.at[c, src], yrecv.at[c, others], rs_recv.at[c])
    plans[3 * C] = (3, lambda dst: s1.at[dst], lambda src, d: orecv.at[src], orecv.at[others], x_got.at[3 * C])
    plans[3 * C + 1] = (4, lambda dst: bsend.at[dst], lambda src, d: brecv.at[src], brecv.at[others], x_got.at[3 * C + 1])
    sent = (nsend.at[:, others], rsend.at[:, others], ysend.at[:, others], s1.at[others], bsend.at[others])

    def x_start(kind):
        group, source, target, _, sem = plans[kind]
        for d in order:
            pltpu.make_async_remote_copy(
                src_ref=source(peer(d)), dst_ref=target(h, d),
                send_sem=x_sent.at[group], recv_sem=sem,
                device_id={"hist": peer(d)}, device_id_type=MESH,
            ).start()

    def x_wait(kind):
        local_wait(*plans[kind][3:])

    def near_plan(c):
        bit = 1 if c % 2 == 0 else max(H // 2, 1)
        return bit, [e for e in range(H) if not e & bit]

    def near_copy(c, to, block, target, sem):
        pltpu.make_async_remote_copy(
            src_ref=nsend.at[c, peer(block)], dst_ref=target,
            send_sem=x_sent.at[0], recv_sem=sem,
            device_id={"hist": peer(to)}, device_id_type=MESH,
        ).start()

    def near_start(c):
        bit, rest = near_plan(c)
        for i, e in enumerate(rest):
            near_copy(c, bit, bit | e, nmid.at[c, i], x_got.at[c])

    def near_middle(c):
        bit, rest = near_plan(c)
        local_wait(nmid.at[c], x_got.at[c])
        for i, e in enumerate(rest):
            nsend[c, peer(e)] += nmid[c, i]
        for i, e in enumerate(rest[1:]):
            near_copy(c, e, e, nrecv.at[c, i], x_got.at[2 * C + c])

    def x_sent_wait(group):
        local_wait(sent[group], x_sent.at[group])

    def gap(chip, q):
        return jnp.where(q > chip, q - 1, q)

    def z_copy(g, st, c, q, where):
        block = g.at[2 * q + core, fine(c), :]
        send, recv, target = {
            "partner": (sp, rp, p * 2 + other),
            "in": (sin, rz, t + 2 * inward),
            "out": (sout, rz, t - 2 * inward),
        }[where]
        slot = (partner_slot(st, c // F), q) if where == "partner" else (st, c, gap(target // 2, q))
        return pltpu.make_async_remote_copy(
            src_ref=block, dst_ref=block,
            send_sem=send.at[st], recv_sem=recv.at[slot],
            device_id={"tcol": target}, device_id_type=MESH,
        )

    def partner_slot(st, c):
        return c if st == 0 else C + c // 2

    def z_partner_wait(g, st, c, n, q):
        step = 1 if st == 0 else 2
        for k in range(c, c + n, step):
            local_wait(g.at[2 * q + other, chunk(k, step), :], rp.at[partner_slot(st, k), q])

    def z_own(g, st, c):
        @pl.when(rim > 0)
        def _():
            z_copy(g, st, c, p, "out").start()

        if Z > 1:
            @pl.when(rim < Z - 1)
            def _():
                z_copy(g, st, c, p, "in").start()

        z_copy(g, st, c, p, "partner").start()

    def exists(side, s):
        return rim < Z - s if side == "in" else rim >= s

    def place(side, s):
        return p + s * inward if side == "in" else p - s * inward

    def z_forward(g, st, side, s, c):
        if s >= (Z if side == "in" else half):
            return

        @pl.when(exists(side, s))
        def _():
            q = place(side, s)
            local_wait(g.at[2 * q + core, fine(c), :], rz.at[st, c, gap(p, q)])
            if side == "in":
                @pl.when(rim > 0)
                def _():
                    z_copy(g, st, c, q, "out").start()
            else:
                z_copy(g, st, c, q, "in").start()
            z_copy(g, st, c, q, "partner").start()

    def z_finish(g, st):
        local_wait(g.at[pl.ds(0, Z)], sp.at[st])
        for k in range(half):
            @pl.when(rim == k)
            def _():
                if k + 1 < Z:
                    local_wait(g.at[pl.ds(0, k + 1)], sin.at[st])
                if k > 0:
                    local_wait(g.at[pl.ds(0, Z - k)], sout.at[st])

    def chip_product(g, acc, q, c, n, first=False):
        at = chunk(c, n)
        m = n * Rc
        left = jnp.concatenate([g[2 * q, at, :], g[2 * q + 1, at, :]], axis=1)
        high, low = halves(left)
        both = mm(jnp.concatenate([high, low], axis=0), ph[pl.ds(2 * q, 2)].reshape(2 * N, N))
        value = both[:m] + both[m:] + mm(high, plo[pl.ds(2 * q, 2)].reshape(2 * N, N))
        if first:
            acc[at, :] = value
        else:
            acc[at, :] += value

    def lane_product(g, acc, b, c, n):
        at = chunk(c, n)
        m = n * Rc
        high, low = halves(g[b, at, :])
        both = mm(jnp.concatenate([high, low], axis=0), ph[b])
        acc[at, :] += both[:m] + both[m:] + mm(high, plo[b])

    def use_lanes(g, st, acc, side, s, c, n):
        if s >= (Z if side == "in" else half):
            return

        @pl.when(exists(side, s))
        def _():
            q = place(side, s)
            lane_product(g, acc, 2 * q + core, c, n)
            z_partner_wait(g, st, c, n, q)
            lane_product(g, acc, 2 * q + other, c, n)

    def use_own(g, st, acc, c, n):
        z_partner_wait(g, st, c, n, p)
        chip_product(g, acc, p, c, n, True)

    def use(g, st, acc, side, s, c, n):
        if s >= (Z if side == "in" else half):
            return

        @pl.when(exists(side, s))
        def _():
            q = place(side, s)
            z_partner_wait(g, st, c, n, q)
            chip_product(g, acc, q, c, n)

    def near(c):
        near_sums(c)
        near_start(c)

    def p_half(k):
        for b in range(k * (T // 2), (k + 1) * (T // 2)):
            p_split(b)

    def gather(g, st, acc, steps, actions):
        for step in steps:
            name = step[0]
            if name in ("in", "out"):
                z_forward(g, st, name, step[1], step[2])
            elif name == "own":
                use_own(g, st, acc, *step[1:])
            elif name == "lanes":
                use_lanes(g, st, acc, *step[1:])
            elif name == "use":
                use(g, st, acc, *step[1:])
            else:
                actions[name](*step[1:])

    def one_steps():
        deep = range(3, Z)
        def hop(s, f):
            yield ("in", s, f)
            if s == 1:
                yield ("out", s, f)

        def far(f):
            for s in deep:
                yield ("in", s, f)

        yield ("begin", 0)
        yield ("near", 0)
        yield ("begin", 1)
        yield ("near", 1)
        yield ("begin", 2)
        yield from hop(1, 0)
        yield ("near", 2)
        yield ("begin", 3)
        yield from hop(1, 1)
        yield ("near", 3)
        yield ("begin", 4)
        yield from hop(1, 2)
        yield ("split", 0)
        yield ("begin", 5)
        yield from hop(2, 0)
        yield ("split", 1)
        yield ("begin", 6)
        yield from hop(1, 3)
        yield from hop(2, 1)
        yield ("begin", 7)
        yield ("own", 0, 2)
        yield from hop(1, 4)
        yield from hop(2, 2)
        yield from far(0)
        yield ("matrices",)
        yield from hop(1, 5)
        yield from hop(2, 3)
        yield from far(1)
        yield ("use", "in", 1, 0, 2)
        yield from hop(1, 6)
        yield from hop(2, 4)
        yield from far(2)
        yield ("use", "out", 1, 0, 2)
        yield ("middle", 0)
        yield ("middle", 1)
        yield from hop(1, 7)
        yield ("use", "in", 2, 0, 2)
        yield ("early", 0)
        yield ("early", 1)
        yield from hop(2, 5)
        yield from far(3)
        for s in range(2, half):
            for f in range(C * F):
                yield ("out", s, f)
            yield ("use", "out", s, 0, C)
        yield ("own", 2, 2)
        yield from hop(2, 6)
        yield ("middle", 2)
        yield ("middle", 3)
        yield from far(4)
        for s in deep:
            yield ("use", "in", s, 0, 2)
        yield ("late", 0)
        yield ("late", 1)
        yield ("use", "in", 1, 2, 2)
        yield ("use", "out", 1, 2, 2)
        yield ("use", "in", 2, 2, 1)
        yield ("early", 2)
        yield from hop(2, 7)
        yield from far(5)
        for s in deep:
            yield ("lanes", "in", s, 2, 1)
        yield ("late", 2)
        yield from far(6)
        yield ("lanes", "in", 2, 3, 1)
        yield ("early", 3)
        yield from far(7)
        for s in deep:
            yield ("lanes", "in", s, 3, 1)
        yield ("late", 3)

    def two_steps():
        for c in range(C):
            yield ("begin", c)
        yield ("rest",)
        yield ("drain", 0)
        yield ("own", 0, C)
        for f in range(6):
            yield ("in", 1, f)
        yield ("out", 1, 0)
        yield ("in", 1, 6)
        yield ("out", 1, 1)
        yield ("in", 1, 7)
        yield ("out", 1, 2)
        yield ("out", 1, 3)
        yield ("use", "in", 1, 0, C)
        for f in range(4, C * F):
            yield ("in", 2, f - 4)
            yield ("out", 1, f)
        for s in range(2, half):
            for f in range(C * F):
                yield ("out", s, f)
            yield ("use", "out", s, 0, C)
        for f in range(C * F - 4, C * F):
            yield ("in", 2, f)
        yield ("drain", 1)
        yield ("use", "out", 1, 0, C)
        for s in range(3, Z):
            for f in range(2 * F):
                yield ("in", s, f)
        for s in range(2, Z):
            yield ("use", "in", s, 0, 2)
        yield ("done", 0)
        yield ("done", 1)
        yield ("use", "in", 2, 2, 2)
        for s in range(3, Z):
            for f in range(2 * F, C * F):
                yield ("in", s, f)
            yield ("lanes", "in", s, 2, 2)
        yield ("done", 2)
        yield ("done", 3)

    for kb in range(nK):
        hist_copy(kb).wait()
        split(hbuf.at[kb], sh.at[kb], sl.at[kb], N, cubic_power, 4)
        if kb == min(2, nK - 1):
            w_split(0, 0)
        if kb + 1 < C:
            w_load(0, kb + 1)
    for kb in range(nK):
        w_step(0, 0, kb)
    for c in range(nK + 1, C):
        w_load(0, c)
    pl.semaphore_wait(barrier, H + 2)
    rs_start(0)
    small[0].start()
    w_load(1, 0)
    small[4].start()
    for c in range(1, C):
        history_sum(0, c)
        rs_start(c)
        w_load(1, c)
    for b in range(nK):
        p_copy(b).start()
    for copy in small[1:4]:
        copy.start()
    small[0].wait()
    small[4].wait()

    def begin_one(f):
        at = inner(f)
        local_wait(rs.at[f // F, :, at, :], rs_recv.at[f])
        total = part[0, f // F, h, at, :] + e1[fine(f), :]
        for d in range(1, H):
            total += rs[f // F, d - 1, at, :]
        pred[fine(f), :] = total
        g1[t, fine(f), :] = cubic_power(total)
        z_own(g1, 0, f)

    def near_sums(c):
        history_sum(1, c)
        part[1, c, h] += e2[chunk(c), :]
        for j in range(H):
            nsend[c, j] = part[1, c, :, :, j * Nh:(j + 1) * Nh]

    def p_split(b):
        p_copy(b).wait()
        split(hbuf.at[b % nK], ph.at[b], plo.at[b], N)
        if b + nK < T:
            p_copy(b + nK).start()

    def split_matrices():
        pltpu.make_async_copy(mat, mat, msem.at[1]).wait()
        split(mat.at[0], ih, il, S)
        split(mat.at[1], kh, kl, S)

        @pl.loop(0, H)
        def _(j):
            for c in range(C):
                at = pl.ds(pl.multiple_of(j * R + c * Rc, Rc), Rc)
                vh[c, j], vl[c, j] = halves(mat[2, at, :])

    def send_right(c):
        value = pred[chunk(c), :] + step_size * acc1[chunk(c), :]
        for j in range(H):
            rsend[c, j] = value[:, j * Nh:(j + 1) * Nh]
        x_start(C + c)
        rf[c, h] = rsend[c, h]

    ahead = rim >= 1 if Z <= 4 else rim >= Z

    def early(c):
        @pl.when(ahead)
        def _():
            send_right(c)

    def late(c):
        @pl.when(jnp.logical_not(ahead))
        def _():
            send_right(c)

    gather(g1, 0, acc1, one_steps(), {
        "near": near, "middle": near_middle, "early": early, "late": late, "begin": begin_one, "split": p_half, "matrices": split_matrices, "done": send_right,
    })

    def pair_store(ref, at, value):
        a, b = halves(value)
        ref[at, :Nh] = a
        ref[at, Nh:] = b

    for c in range(C):
        x_wait(C + c)
        for j in range(H):
            pair_store(x2, pl.ds(j * R + c * Rc, Rc), rf[c, j])

    def apply(high, low, source):
        wide = mm(high, source[...])
        return wide[:, :Nh] + wide[:, Nh:] + mm(low, source[:, :Nh])

    value = apply(ih[...], il[...], x2)
    s1[...] = value.reshape(H, R, Nh)
    pair_store(q2, pl.ds(0, S), cubic_power(value))

    for c in range(C):
        if H > 2:
            local_wait(nrecv.at[c], x_got.at[2 * C + c])
    value = apply(kh[...], kl[...], q2)
    base = []
    for j in range(H):
        for c in range(C):
            total = nsend[c, h, j]
            if H > 2:
                for i in range(H // 2 - 1):
                    total += nrecv[c, i, j]
            base.append(total)
    value += jnp.concatenate(base, axis=0)
    pair_store(r2, pl.ds(0, S), step_size * cubic_power(value))
    pair_store(t2, pl.ds(0, S), value)

    for c in range(C):
        value = apply(vh[c].reshape(H * Rc, S), vl[c].reshape(H * Rc, S), r2)
        ysend[c] = value.reshape(H, Rc, Nh)
        x_start(2 * C + c)
        yrecv[c, h] = ysend[c, h]
    for c in range(C):
        value = apply(vh[c].reshape(H * Rc, S), vl[c].reshape(H * Rc, S), t2)
        bsend[:, chunk(c), :] = value.reshape(H, Rc, Nh)

    def begin_two(c):
        x_wait(2 * C + c)
        g2[t, chunk(c), :] = jnp.concatenate([yrecv[c, j] for j in range(H)], axis=1)
        for f in range(c * F, c * F + F):
            z_own(g2, 1, f)

    def rest():
        zero_ref[...] = jnp.zeros(zero_ref.shape, f32)
        x_start(3 * C)
        orecv[h] = s1[h]
        x_start(3 * C + 1)
        brecv[h] = bsend[h]

    def drain_one():
        local_wait(part.at[0, :, others], rs_send)
        z_finish(g1, 0)
        x_sent_wait(0)
        x_sent_wait(1)

    def drain_two():
        x_wait(3 * C)
        for j in range(H):
            o1_ref[:, j * Nh:(j + 1) * Nh] = orecv[j]
        x_wait(3 * C + 1)
        for group in (2, 3, 4):
            x_sent_wait(group)

    def finish(c):
        at = chunk(c)
        o2_ref[at, :] = acc2[at, :] + jnp.concatenate([brecv[j, at, :] for j in range(H)], axis=1)

    gather(g2, 1, acc2, two_steps(), {
        "begin": begin_two, "rest": rest, "drain": lambda k: (drain_one, drain_two)[k](), "done": finish,
    })
    z_finish(g2, 1)


def shards(*operands):
    history, w1, w2 = operands[:3]
    K, N = history.shape
    S = w1.shape[0]
    H, T, C = lax.axis_size("hist"), lax.axis_size("tcol"), 4
    R = S // H
    Rc, Nh, nK, Z = R // C, N // H, K // N, T // 2
    split_rows = lambda w: w.reshape(H, R, K)
    V, D = pltpu.VMEM, pltpu.SemaphoreType.DMA
    first, second, zero = pl.pallas_call(
        functools.partial(kernel, H, T, C),
        out_shape=[pltpu.VMEM((R, N), f32), pltpu.VMEM((R, N), f32), pltpu.VMEM((1, N), f32)],
        in_specs=[pl.BlockSpec(memory_space=pl.ANY)] * 9,
        out_specs=[pl.BlockSpec(memory_space=pltpu.VMEM)] * 3,
        scratch_shapes=[
            V((nK, N, N), f32), V((2, C, H, Rc, K), f32),
            V((H, Rc, K), bf16), V((H, Rc, K), bf16),
            V((nK, N, N), bf16), V((nK, N, N), bf16),
            V((T, N, N), bf16), V((T, N, N), bf16),
            V((3, S, S), f32),
            *[V((S, S), bf16)] * 4, *[V((C, H, Rc, S), bf16)] * 2,
            V((R, N), f32), V((R, N), f32),
            V((2, C, H, Rc, N), f32), V((C, H - 1, Rc, N), f32),
            V((R, N), f32), V((R, N), f32), V((R, N), f32),
            V((T, R, N), f32), V((T, R, N), f32),
            V((C, H, H, Rc, Nh), f32), V((C, H // 2, H, Rc, Nh), f32), V((C, max(H // 2 - 1, 1), H, Rc, Nh), f32),
            V((C, H, Rc, Nh), f32), V((C, H, Rc, Nh), f32),
            V((H, R, Nh), f32), V((H, R, Nh), f32),
            V((C, H, Rc, Nh), f32), V((C, H, Rc, Nh), f32),
            V((H, R, Nh), f32), V((H, R, Nh), f32),
            *[V((S, 2 * Nh), bf16)] * 4,
            D((nK,)), D((C,)), D((3,)),
            D, D((2 * C,)), D((5,)), D((3 * C + 2,)),
            D((2,)), D((2,)), D((2,)), D((2, 2 * C, max(Z - 1, 1))), D((C + C // 2, Z)),
        ],
        compiler_params=pltpu.CompilerParams(
            collective_id=0, has_side_effects=True, vmem_limit_bytes=63 * 1024 * 1024
        ),
    )(history, split_rows(w1), split_rows(w2), *operands[3:])
    return first + zero, second + zero


def solution(mesh):
    return jax.shard_map(
        shards,
        mesh=mesh,
        in_specs=(
            P("hist", "tcol"),
            P(None, "hist"),
            P(None, "hist"),
            P(),
            P(None, "tcol"),
            P(),
            P(),
            P(None, "tcol"),
            P(None, "tcol"),
        ),
        out_specs=(P("hist", "tcol"), P("hist", "tcol")),
        check_vma=False,
    )
```

```python
import functools

import jax
import jax.numpy as jnp
from jax import lax
from jax.experimental import pallas as pl
from jax.experimental.pallas import tpu as pltpu
from jax.sharding import PartitionSpec as P

strength = 0.2
step_size = 0.5
MESH = pl.DeviceIdType.MESH
f32 = jnp.float32
bf16 = jnp.bfloat16


def cubic_power(value):
    return strength * value * value * value


def halves(value):
    high = value.astype(bf16)
    return high, (value - high.astype(f32)).astype(bf16)


def mm(left, right):
    return jnp.dot(left, right, preferred_element_type=f32)


def kernel(
    H, T, C,
    hist_ref, w1_ref, w2_ref, link_ref, prop_ref, inv1_ref, inv2_ref, e1_ref, e2_ref,
    o1_ref, o2_ref, zero_ref,
    hbuf, wbuf, wh, wl, sh, sl, ph, plo, mat, ih, il, kh, kl, vh, vl, e1, e2,
    part, rs, pred, acc1, acc2, g1, g2, nsend, nmid, nrecv, rsend, rf, s1, orecv,
    ysend, yrecv, bsend, brecv, s1near, x2, q2, r2, t2,
    hsem, wsem, msem, rs_send, rs_recv, x_sent, x_got,
    sp, sin, sout, rz, rp,
):
    K, N = hist_ref.shape
    R = w1_ref.shape[1]
    S = R * H
    Rc = R // C
    F = 2
    Rf = Rc // F
    Nh = N // H
    nK = K // N
    Z = T // 2
    h = lax.axis_index("hist")
    t = lax.axis_index("tcol")
    p = t // 2
    core = t % 2
    other = 1 - core
    half = (Z + 1) // 2
    upper = p // half
    inward = 1 - 2 * upper
    rim = p + upper * (Z - 1 - 2 * p)
    tile = 32

    def peer(d):
        if H & (H - 1):
            return None
        value, bit = h, 1
        while bit < H:
            if d & bit:
                value = value + bit * (1 - 2 * ((h // bit) % 2))
            bit *= 2
        return value

    order = sorted(range(1, H), key=lambda d: -bin(d).count("1"))

    def split(source, high, low, rows, function=lambda v: v, unroll=1):
        @pl.loop(0, rows // tile, unroll=unroll)
        def _(i):
            at = pl.ds(pl.multiple_of(i * tile, tile), tile)
            a, b = halves(function(source[at, :]))
            high[at, :] = a
            low[at, :] = b

    def chunk(c, n=1):
        return pl.ds(c * Rc, n * Rc)

    def fine(f):
        return pl.ds(f * Rf, Rf)

    def inner(f):
        return pl.ds(f % F * Rf, Rf)

    def hist_copy(kb):
        return pltpu.make_async_copy(hist_ref.at[pl.ds(kb * N, N), :], hbuf.at[kb], hsem.at[kb])

    def w_copy(w, c):
        ref = (w1_ref, w2_ref)[w]
        return pltpu.make_async_copy(ref.at[:, chunk(c), :], wbuf.at[w, c], wsem.at[c])

    def w_load(w, c):
        w_copy(w, c).start()

    def p_copy(b):
        return pltpu.make_async_copy(
            prop_ref.at[pl.ds(b * N, N), :], hbuf.at[b % nK], hsem.at[b % nK]
        )

    own_rows = pl.ds(pl.multiple_of(h * R, R), R)
    small = (
        pltpu.make_async_copy(e1_ref.at[own_rows, :], e1, msem.at[0]),
        pltpu.make_async_copy(inv1_ref, mat.at[0], msem.at[1]),
        pltpu.make_async_copy(link_ref, mat.at[1], msem.at[1]),
        pltpu.make_async_copy(inv2_ref, mat.at[2], msem.at[1]),
        pltpu.make_async_copy(e2_ref.at[own_rows, :], e2, msem.at[2]),
    )

    hist_copy(0).start()
    w_load(0, 0)
    for kb in range(1, nK):
        hist_copy(kb).start()

    barrier = pltpu.get_barrier_semaphore()

    def greet(device):
        pl.semaphore_signal(barrier, inc=1, device_id=device, device_id_type=MESH)

    for d in range(1, H):
        greet({"hist": peer(d)})
    greet({"tcol": p * 2 + other})
    greet({"tcol": lax.rem(p + 1, Z) * 2 + core})
    greet({"tcol": lax.rem(p + Z - 1, Z) * 2 + core})

    def w_split(w, c):
        w_copy(w, c).wait()
        step = 16

        @pl.loop(0, H)
        def _(j):
            for i in range(Rc // step):
                at = pl.ds(i * step, step)
                wh[j, at, :], wl[j, at, :] = halves(wbuf[w, c, j, at, :])

    def w_step(w, c, kb):
        cols = pl.ds(kb * N, N)
        a = wh[:, :, cols].reshape(H * Rc, N)
        b = wl[:, :, cols].reshape(H * Rc, N)
        value = mm(a, sh[kb]) + mm(b, sh[kb]) + mm(a, sl[kb])
        value = value.reshape(H, Rc, N)
        if kb == 0:
            part[w, c] = value
        else:
            part[w, c] += value

    def history_sum(w, c):
        w_split(w, c)
        for kb in range(nK):
            w_step(w, c, kb)

    def rs_copy(f, d):
        return pltpu.make_async_remote_copy(
            src_ref=part.at[0, f // F, peer(d), inner(f), :], dst_ref=rs.at[f // F, d - 1, inner(f), :],
            send_sem=rs_send, recv_sem=rs_recv.at[f],
            device_id={"hist": peer(d)}, device_id_type=MESH,
        )

    def rs_start(c):
        for f in range(c * F, c * F + F):
            for d in order:
                rs_copy(f, d).start()

    def local_wait(ref, sem):
        pltpu.make_async_copy(ref, ref, sem).wait()

    others = pl.ds(0, H - 1)
    plans = {}
    for c in range(C):
        plans[C + c] = (
            1, lambda dst, c=c: rsend.at[c, dst], lambda src, d, c=c: rf.at[c, src], rf.at[c, others], x_got.at[C + c])
    for f in range(C * F):
        plans["y", f] = (
            2, lambda dst, f=f: ysend.at[f // F, dst, inner(f), :],
            lambda src, d, f=f: yrecv.at[f // F, src, inner(f), :],
            yrecv.at[f // F, others, inner(f), :], rs_recv.at[f])
    plans[3 * C] = (3, lambda dst: s1.at[dst], lambda src, d: orecv.at[src], orecv.at[others], x_got.at[3 * C])
    plans[3 * C + 1] = (4, lambda dst: bsend.at[dst], lambda src, d: brecv.at[src], brecv.at[others], x_got.at[3 * C + 1])
    sent = (nsend.at[:, others], rsend.at[:, others], ysend.at[:, others], s1.at[others], bsend.at[others])

    def x_start(kind):
        group, source, target, _, sem = plans[kind]
        for d in order:
            pltpu.make_async_remote_copy(
                src_ref=source(peer(d)), dst_ref=target(h, d),
                send_sem=x_sent.at[group], recv_sem=sem,
                device_id={"hist": peer(d)}, device_id_type=MESH,
            ).start()

    def x_wait(kind):
        local_wait(*plans[kind][3:])

    def near_plan(c):
        bit = 1 if c % 2 == 0 else max(H // 2, 1)
        return bit, [e for e in range(H) if not e & bit]

    def near_copy(c, to, block, target, sem):
        pltpu.make_async_remote_copy(
            src_ref=nsend.at[c, peer(block)], dst_ref=target,
            send_sem=x_sent.at[0], recv_sem=sem,
            device_id={"hist": peer(to)}, device_id_type=MESH,
        ).start()

    def near_start(c):
        bit, rest = near_plan(c)
        for i, e in enumerate(rest):
            near_copy(c, bit, bit | e, nmid.at[c, i], x_got.at[c])

    def near_middle(c):
        bit, rest = near_plan(c)
        local_wait(nmid.at[c], x_got.at[c])
        for i, e in enumerate(rest):
            nsend[c, peer(e)] += nmid[c, i]
        for i, e in enumerate(rest[1:]):
            near_copy(c, e, e, nrecv.at[c, i], x_got.at[2 * C + c])

    def x_sent_wait(group):
        local_wait(sent[group], x_sent.at[group])

    def gap(chip, q):
        return jnp.where(q > chip, q - 1, q)

    def z_copy(g, st, c, q, where):
        block = g.at[2 * q + core, fine(c), :]
        send, recv, target = {
            "partner": (sp, rp, p * 2 + other),
            "in": (sin, rz, t + 2 * inward),
            "out": (sout, rz, t - 2 * inward),
        }[where]
        slot = (partner_slot(st, c // F), q) if where == "partner" else (st, c, gap(target // 2, q))
        return pltpu.make_async_remote_copy(
            src_ref=block, dst_ref=block,
            send_sem=send.at[st], recv_sem=recv.at[slot],
            device_id={"tcol": target}, device_id_type=MESH,
        )

    def partner_slot(st, c):
        return c if st == 0 else C + c // 2

    ahead = rim >= 1 if Z <= 4 else rim >= Z

    def z_partner_wait(g, st, c, n, q):
        step = 1 if st == 0 else 2
        for k in range(c, c + n, step):
            local_wait(g.at[2 * q + other, chunk(k, step), :], rp.at[partner_slot(st, k), q])

    def z_own(g, st, c):
        @pl.when(rim > 0)
        def _():
            z_copy(g, st, c, p, "out").start()

        if Z > 1:
            @pl.when(rim < Z - 1)
            def _():
                z_copy(g, st, c, p, "in").start()

        z_copy(g, st, c, p, "partner").start()

    def exists(side, s):
        return rim < Z - s if side == "in" else rim >= s

    def place(side, s):
        return p + s * inward if side == "in" else p - s * inward

    def z_forward(g, st, side, s, c):
        if s >= (Z if side == "in" else half):
            return

        @pl.when(exists(side, s))
        def _():
            q = place(side, s)
            local_wait(g.at[2 * q + core, fine(c), :], rz.at[st, c, gap(p, q)])
            if side == "in":
                @pl.when(rim > 0)
                def _():
                    z_copy(g, st, c, q, "out").start()
            else:
                z_copy(g, st, c, q, "in").start()
            z_copy(g, st, c, q, "partner").start()

    def z_finish(g, st):
        local_wait(g.at[pl.ds(0, Z)], sp.at[st])
        for k in range(half):
            @pl.when(rim == k)
            def _():
                if k + 1 < Z:
                    local_wait(g.at[pl.ds(0, k + 1)], sin.at[st])
                if k > 0:
                    local_wait(g.at[pl.ds(0, Z - k)], sout.at[st])

    def lane_product(g, acc, b, c, n, first=False):
        at = chunk(c, n)
        m = n * Rc
        high, low = halves(g[b, at, :])
        both = mm(jnp.concatenate([high, low], axis=0), ph[b])
        value = both[:m] + both[m:] + mm(high, plo[b])
        if first:
            acc[at, :] = value
        else:
            acc[at, :] += value

    def use_own(g, st, acc):
        lane_product(g, acc, t, 0, C, True)

    def partner_own(g, st, acc):
        z_partner_wait(g, st, 0, C, p)
        lane_product(g, acc, 2 * p + other, 0, C)

    def use(g, st, acc, side, s, c, n):
        if s >= (Z if side == "in" else half):
            return

        @pl.when(exists(side, s))
        def _():
            lane_product(g, acc, 2 * place(side, s) + core, c, n)

    def partner_use(g, st, acc, side, s, c, n):
        if s >= (Z if side == "in" else half):
            return

        @pl.when(exists(side, s))
        def _():
            q = place(side, s)
            z_partner_wait(g, st, c, n, q)
            lane_product(g, acc, 2 * q + other, c, n)

    def near(c):
        near_sums(c)
        near_start(c)

    def p_half(k):
        for b in range(k * (T // 2), (k + 1) * (T // 2)):
            p_split(b)

    def gather(g, st, acc, steps, actions):
        for step in steps:
            name = step[0]
            if name in ("in", "out"):
                z_forward(g, st, name, step[1], step[2])
            elif name == "own":
                use_own(g, st, acc)
            elif name == "partner":
                partner_own(g, st, acc)
            elif name in ("ahead", "behind"):
                @pl.when(ahead if name == "ahead" else jnp.logical_not(ahead))
                def _():
                    partner_use(g, st, acc, *step[1:])
            elif name == "use":
                use(g, st, acc, *step[1:])
            elif name == "other":
                partner_use(g, st, acc, *step[1:])
            else:
                actions[name](*step[1:])

    def one_steps():
        deep = range(3, Z)
        def hop(s, f):
            yield ("in", s, f)
            if s == 1:
                yield ("out", s, f)

        def far(f):
            for s in deep:
                yield ("in", s, f)

        yield ("begin", 0)
        yield ("near", 0)
        yield ("begin", 1)
        yield ("near", 1)
        yield ("begin", 2)
        yield from hop(1, 0)
        yield ("near", 2)
        yield ("begin", 3)
        yield from hop(1, 1)
        yield ("split", 0)
        yield ("begin", 4)
        yield from hop(1, 2)
        yield ("near", 3)
        yield ("begin", 5)
        yield from hop(2, 0)
        yield ("split", 1)
        yield ("begin", 6)
        yield from hop(1, 3)
        yield from hop(2, 1)
        yield ("begin", 7)
        yield ("own",)
        yield from hop(1, 4)
        yield from hop(2, 2)
        yield from far(0)
        yield from hop(1, 5)
        yield from hop(2, 3)
        yield from far(1)
        yield ("use", "in", 1, 0, 2)
        yield from hop(1, 6)
        yield from hop(2, 4)
        yield from far(2)
        yield ("use", "out", 1, 0, 2)
        yield ("middle", 0)
        yield ("middle", 1)
        yield from hop(1, 7)
        yield ("use", "in", 2, 0, 2)
        yield from hop(2, 5)
        yield from far(3)
        yield ("use", "in", 1, 2, 2)
        yield ("use", "out", 1, 2, 2)
        yield ("partner",)
        for s in range(2, half):
            for f in range(C * F):
                yield ("out", s, f)
            yield ("use", "out", s, 0, C)
            yield ("other", "out", s, 0, C)
        yield from hop(2, 6)
        yield ("middle", 2)
        yield ("middle", 3)
        yield from far(4)
        yield ("other", "in", 1, 0, C)
        yield ("other", "out", 1, 0, C)
        yield ("other", "in", 2, 0, 2)
        yield ("early", 0)
        yield ("early", 1)
        for s in deep:
            yield ("use", "in", s, 0, 2)
        yield from hop(2, 7)
        yield from far(5)
        yield ("use", "in", 2, 2, 2)
        yield ("ahead", "in", 2, 2, 1)
        yield ("early", 2)
        yield ("ahead", "in", 2, 3, 1)
        yield ("early", 3)
        yield from far(6)
        for s in deep:
            yield ("other", "in", s, 0, 2)
        yield ("late", 0)
        yield ("late", 1)
        yield from far(7)
        yield ("behind", "in", 2, 2, 2)
        for c in (2, 3):
            for s in deep:
                yield ("use", "in", s, c, 1)
                yield ("other", "in", s, c, 1)
            yield ("late", c)
        yield ("matrices",)

    def two_steps():
        for c in range(C):
            yield ("begin", c)
        yield ("rest",)
        yield ("drain", 0)
        yield ("own",)
        for f in range(6):
            yield ("in", 1, f)
        yield ("out", 1, 0)
        yield ("in", 1, 6)
        yield ("out", 1, 1)
        yield ("in", 1, 7)
        yield ("out", 1, 2)
        yield ("out", 1, 3)
        yield ("use", "in", 1, 0, C)
        for f in range(4, C * F):
            yield ("in", 2, f - 4)
            yield ("out", 1, f)
        for s in range(2, half):
            for f in range(C * F):
                yield ("out", s, f)
            yield ("use", "out", s, 0, C)
            yield ("other", "out", s, 0, C)
        for f in range(C * F - 4, C * F):
            yield ("in", 2, f)
        yield ("drain", 1)
        deep = range(3, Z)

        def far(f):
            for s in deep:
                yield ("in", s, f)

        yield ("use", "out", 1, 0, C)
        yield from far(0)
        yield ("partner",)
        yield from far(1)
        yield ("other", "in", 1, 0, C)
        yield from far(2)
        yield ("other", "out", 1, 0, C)
        yield ("use", "in", 2, 0, C)
        yield from far(3)
        yield from far(4)
        for s in deep:
            yield ("use", "in", s, 0, 2)
        yield from far(5)
        yield ("other", "in", 2, 0, C)
        yield from far(6)
        yield from far(7)
        for s in deep:
            yield ("use", "in", s, 2, 2)
            yield ("other", "in", s, 0, 2)
        yield ("done", 0)
        yield ("done", 1)
        for s in deep:
            yield ("other", "in", s, 2, 2)
        yield ("done", 2)
        yield ("done", 3)

    for kb in range(nK):
        hist_copy(kb).wait()
        split(hbuf.at[kb], sh.at[kb], sl.at[kb], N, cubic_power, 4)
        if kb == min(2, nK - 1):
            w_split(0, 0)
        if kb + 1 < C:
            w_load(0, kb + 1)
    for kb in range(nK):
        w_step(0, 0, kb)
    for c in range(nK + 1, C):
        w_load(0, c)
    pl.semaphore_wait(barrier, H + 2)
    rs_start(0)
    small[0].start()
    w_load(1, 0)
    small[4].start()
    for c in range(1, C):
        history_sum(0, c)
        rs_start(c)
        w_load(1, c)
    for b in range(nK):
        p_copy(b).start()
    for copy in small[1:4]:
        copy.start()
    small[0].wait()
    small[4].wait()

    def begin_one(f):
        at = inner(f)
        local_wait(rs.at[f // F, :, at, :], rs_recv.at[f])
        total = part[0, f // F, h, at, :] + e1[fine(f), :]
        for d in range(1, H):
            total += rs[f // F, d - 1, at, :]
        pred[fine(f), :] = total
        g1[t, fine(f), :] = cubic_power(total)
        z_own(g1, 0, f)

    def near_sums(c):
        history_sum(1, c)
        part[1, c, h] += e2[chunk(c), :]
        for j in range(H):
            nsend[c, j] = part[1, c, :, :, j * Nh:(j + 1) * Nh]

    def p_split(b):
        p_copy(b).wait()
        split(hbuf.at[b % nK], ph.at[b], plo.at[b], N)
        if b + nK < T:
            p_copy(b + nK).start()

    def split_matrices():
        pltpu.make_async_copy(mat, mat, msem.at[1]).wait()
        split(mat.at[0], ih, il, S)
        split(mat.at[1], kh, kl, S)

        @pl.loop(0, H)
        def _(j):
            for c in range(C):
                at = pl.ds(pl.multiple_of(j * R + c * Rc, Rc), Rc)
                vh[c, j], vl[c, j] = halves(mat[2, at, :])

    def send_right(c):
        value = pred[chunk(c), :] + step_size * acc1[chunk(c), :]
        for j in range(H):
            rsend[c, j] = value[:, j * Nh:(j + 1) * Nh]
        x_start(C + c)
        rf[c, h] = rsend[c, h]

    def early(c):
        @pl.when(ahead)
        def _():
            send_right(c)

    def late(c):
        @pl.when(jnp.logical_not(ahead))
        def _():
            send_right(c)

    gather(g1, 0, acc1, one_steps(), {
        "near": near, "middle": near_middle, "early": early, "late": late, "begin": begin_one, "split": p_half, "matrices": split_matrices, "done": send_right,
    })

    def pair_store(ref, at, value):
        a, b = halves(value)
        ref[at, :Nh] = a
        ref[at, Nh:] = b

    def near_sum():
        for c in range(C):
            if H > 2:
                local_wait(nrecv.at[c], x_got.at[2 * C + c])
            total = nsend[c, h]
            if H > 2:
                for i in range(H // 2 - 1):
                    total += nrecv[c, i]
            s1near[:, chunk(c), :] = total

    for c in range(C):
        x_wait(C + c)
        if c == C // 2 - 1:
            near_sum()
        for j in range(H):
            pair_store(x2, pl.ds(j * R + c * Rc, Rc), rf[c, j])

    def apply(high, low, source):
        wide = mm(high, source[...])
        return wide[:, :Nh] + wide[:, Nh:] + mm(low, source[:, :Nh])

    value = apply(ih[...], il[...], x2)
    s1[...] = value.reshape(H, R, Nh)
    pair_store(q2, pl.ds(0, S), cubic_power(value))

    value = apply(kh[...], kl[...], q2)
    value += s1near[...].reshape(S, Nh)
    pair_store(r2, pl.ds(0, S), step_size * cubic_power(value))
    pair_store(t2, pl.ds(0, S), value)

    for c in range(C):
        value = apply(vh[c].reshape(H * Rc, S), vl[c].reshape(H * Rc, S), r2)
        ysend[c] = value.reshape(H, Rc, Nh)
        for f in range(c * F, c * F + F):
            x_start(("y", f))
        yrecv[c, h] = ysend[c, h]
    for c in range(C):
        value = apply(vh[c].reshape(H * Rc, S), vl[c].reshape(H * Rc, S), t2)
        bsend[:, chunk(c), :] = value.reshape(H, Rc, Nh)

    def begin_two(c):
        for f in range(c * F, c * F + F):
            x_wait(("y", f))
            g2[t, fine(f), :] = jnp.concatenate([yrecv[c, j, inner(f), :] for j in range(H)], axis=1)
            z_own(g2, 1, f)

    def rest():
        zero_ref[...] = jnp.zeros(zero_ref.shape, f32)
        x_start(3 * C)
        orecv[h] = s1[h]
        x_start(3 * C + 1)
        brecv[h] = bsend[h]

    def drain_one():
        local_wait(part.at[0, :, others], rs_send)
        z_finish(g1, 0)
        x_sent_wait(0)
        x_sent_wait(1)

    def drain_two():
        x_wait(3 * C)
        for j in range(H):
            o1_ref[:, j * Nh:(j + 1) * Nh] = orecv[j]
        x_wait(3 * C + 1)
        for group in (2, 3, 4):
            x_sent_wait(group)

    def finish(c):
        at = chunk(c)
        o2_ref[at, :] = acc2[at, :] + jnp.concatenate([brecv[j, at, :] for j in range(H)], axis=1)

    gather(g2, 1, acc2, two_steps(), {
        "begin": begin_two, "rest": rest, "drain": lambda k: (drain_one, drain_two)[k](), "done": finish,
    })
    z_finish(g2, 1)


def shards(*operands):
    history, w1, w2 = operands[:3]
    K, N = history.shape
    S = w1.shape[0]
    H, T, C = lax.axis_size("hist"), lax.axis_size("tcol"), 4
    R = S // H
    Rc, Nh, nK, Z = R // C, N // H, K // N, T // 2
    split_rows = lambda w: w.reshape(H, R, K)
    V, D = pltpu.VMEM, pltpu.SemaphoreType.DMA
    first, second, zero = pl.pallas_call(
        functools.partial(kernel, H, T, C),
        out_shape=[pltpu.VMEM((R, N), f32), pltpu.VMEM((R, N), f32), pltpu.VMEM((1, N), f32)],
        in_specs=[pl.BlockSpec(memory_space=pl.ANY)] * 9,
        out_specs=[pl.BlockSpec(memory_space=pltpu.VMEM)] * 3,
        scratch_shapes=[
            V((nK, N, N), f32), V((2, C, H, Rc, K), f32),
            V((H, Rc, K), bf16), V((H, Rc, K), bf16),
            V((nK, N, N), bf16), V((nK, N, N), bf16),
            V((T, N, N), bf16), V((T, N, N), bf16),
            V((3, S, S), f32),
            *[V((S, S), bf16)] * 4, *[V((C, H, Rc, S), bf16)] * 2,
            V((R, N), f32), V((R, N), f32),
            V((2, C, H, Rc, N), f32), V((C, H - 1, Rc, N), f32),
            V((R, N), f32), V((R, N), f32), V((R, N), f32),
            V((T, R, N), f32), V((T, R, N), f32),
            V((C, H, H, Rc, Nh), f32), V((C, H // 2, H, Rc, Nh), f32), V((C, max(H // 2 - 1, 1), H, Rc, Nh), f32),
            V((C, H, Rc, Nh), f32), V((C, H, Rc, Nh), f32),
            V((H, R, Nh), f32), V((H, R, Nh), f32),
            V((C, H, Rc, Nh), f32), V((C, H, Rc, Nh), f32),
            V((H, R, Nh), f32), V((H, R, Nh), f32), V((H, R, Nh), f32),
            *[V((S, 2 * Nh), bf16)] * 4,
            D((nK,)), D((C,)), D((3,)),
            D, D((2 * C,)), D((5,)), D((3 * C + 2,)),
            D((2,)), D((2,)), D((2,)), D((2, 2 * C, max(Z - 1, 1))), D((C + C // 2, Z)),
        ],
        compiler_params=pltpu.CompilerParams(
            collective_id=0, has_side_effects=True, vmem_limit_bytes=63 * 1024 * 1024
        ),
    )(history, split_rows(w1), split_rows(w2), *operands[3:])
    return first + zero, second + zero


def solution(mesh):
    return jax.shard_map(
        shards,
        mesh=mesh,
        in_specs=(
            P("hist", "tcol"),
            P(None, "hist"),
            P(None, "hist"),
            P(),
            P(None, "tcol"),
            P(),
            P(),
            P(None, "tcol"),
            P(None, "tcol"),
        ),
        out_specs=(P("hist", "tcol"), P("hist", "tcol")),
        check_vma=False,
    )
```

```python
import functools

import jax
import jax.numpy as jnp
from jax import lax
from jax.experimental import pallas as pl
from jax.experimental.pallas import tpu as pltpu
from jax.sharding import PartitionSpec as P

strength = 0.2
step_size = 0.5
MESH = pl.DeviceIdType.MESH
f32 = jnp.float32
bf16 = jnp.bfloat16


def cubic_power(value):
    return strength * value * value * value


def halves(value):
    high = value.astype(bf16)
    return high, (value - high.astype(f32)).astype(bf16)


def mm(left, right):
    return jnp.dot(left, right, preferred_element_type=f32)


def kernel(
    H, T, C,
    hist_ref, w1_ref, w2_ref, link_ref, prop_ref, inv1_ref, inv2_ref, e1_ref, e2_ref,
    o1_ref, o2_ref, zero_ref,
    hbuf, wbuf, wh, wl, sh, sl, ph, plo, mat, ih, il, kh, kl, vh, vl, e1, e2,
    part, rs, pred, acc1, acc2, g1, g2, nsend, nmid, nrecv, rsend, rf, s1, orecv,
    ysend, yrecv, bsend, brecv, s1near, x2, q2, r2, t2,
    hsem, wsem, msem, rs_send, rs_recv, x_sent, x_got,
    sp, sin, sout, rz, rp,
):
    K, N = hist_ref.shape
    R = w1_ref.shape[1]
    S = R * H
    Rc = R // C
    F = 2
    Rf = Rc // F
    Nh = N // H
    nK = K // N
    Z = T // 2
    h = lax.axis_index("hist")
    t = lax.axis_index("tcol")
    p = t // 2
    core = t % 2
    other = 1 - core
    half = (Z + 1) // 2
    upper = p // half
    inward = 1 - 2 * upper
    rim = p + upper * (Z - 1 - 2 * p)
    tile = 32

    def peer(d):
        if H & (H - 1):
            return None
        value, bit = h, 1
        while bit < H:
            if d & bit:
                value = value + bit * (1 - 2 * ((h // bit) % 2))
            bit *= 2
        return value

    order = sorted(range(1, H), key=lambda d: -bin(d).count("1"))

    def split(source, high, low, rows, function=lambda v: v, unroll=1):
        @pl.loop(0, rows // tile, unroll=unroll)
        def _(i):
            at = pl.ds(pl.multiple_of(i * tile, tile), tile)
            a, b = halves(function(source[at, :]))
            high[at, :] = a
            low[at, :] = b

    def chunk(c, n=1):
        return pl.ds(c * Rc, n * Rc)

    def fine(f):
        return pl.ds(f * Rf, Rf)

    def inner(f):
        return pl.ds(f % F * Rf, Rf)

    def hist_copy(kb):
        return pltpu.make_async_copy(hist_ref.at[pl.ds(kb * N, N), :], hbuf.at[kb], hsem.at[kb])

    def w_load(w, c):
        ref = (w1_ref, w2_ref)[w]
        for j in range(H):
            pltpu.make_async_copy(ref.at[j, chunk(c), :], wbuf.at[w, c, j], wsem.at[c]).start()

    def p_copy(b):
        return pltpu.make_async_copy(
            prop_ref.at[pl.ds(b * N, N), :], hbuf.at[b % nK], hsem.at[b % nK]
        )

    own_rows = pl.ds(pl.multiple_of(h * R, R), R)
    small = (
        pltpu.make_async_copy(e1_ref.at[own_rows, :], e1, msem.at[0]),
        pltpu.make_async_copy(inv1_ref, mat.at[0], msem.at[1]),
        pltpu.make_async_copy(link_ref, mat.at[1], msem.at[1]),
        pltpu.make_async_copy(inv2_ref, mat.at[2], msem.at[1]),
        pltpu.make_async_copy(e2_ref.at[own_rows, :], e2, msem.at[2]),
    )

    hist_copy(0).start()
    w_load(0, 0)
    for kb in range(1, nK):
        hist_copy(kb).start()

    barrier = pltpu.get_barrier_semaphore()

    def greet(device):
        pl.semaphore_signal(barrier, inc=1, device_id=device, device_id_type=MESH)

    for d in range(1, H):
        greet({"hist": peer(d)})
    greet({"tcol": p * 2 + other})
    greet({"tcol": lax.rem(p + 1, Z) * 2 + core})
    greet({"tcol": lax.rem(p + Z - 1, Z) * 2 + core})

    def w_split(w, c):
        local_wait(wbuf.at[w, c], wsem.at[c])
        step = 16

        @pl.loop(0, H)
        def _(j):
            for i in range(Rc // step):
                at = pl.ds(i * step, step)
                wh[j, at, :], wl[j, at, :] = halves(wbuf[w, c, j, at, :])

    def w_step(w, c, kb):
        cols = pl.ds(kb * N, N)
        a = wh[:, :, cols].reshape(H * Rc, N)
        b = wl[:, :, cols].reshape(H * Rc, N)
        value = mm(a, sh[kb]) + mm(b, sh[kb]) + mm(a, sl[kb])
        value = value.reshape(H, Rc, N)
        if kb == 0:
            part[w, c] = value
        else:
            part[w, c] += value

    def history_sum(w, c):
        w_split(w, c)
        for kb in range(nK):
            w_step(w, c, kb)

    def rs_copy(f, d):
        return pltpu.make_async_remote_copy(
            src_ref=part.at[0, f // F, peer(d), inner(f), :], dst_ref=rs.at[f // F, d - 1, inner(f), :],
            send_sem=rs_send, recv_sem=rs_recv.at[f],
            device_id={"hist": peer(d)}, device_id_type=MESH,
        )

    def rs_start(c):
        for f in range(c * F, c * F + F):
            for d in order:
                rs_copy(f, d).start()

    def local_wait(ref, sem):
        pltpu.make_async_copy(ref, ref, sem).wait()

    others = pl.ds(0, H - 1)
    plans = {}
    for c in range(C):
        plans[C + c] = (
            1, lambda dst, c=c: rsend.at[c, dst], lambda src, d, c=c: rf.at[c, src], rf.at[c, others], x_got.at[C + c])
    for f in range(C * F):
        plans["y", f] = (
            2, lambda dst, f=f: ysend.at[f // F, dst, inner(f), :],
            lambda src, d, f=f: yrecv.at[f // F, src, inner(f), :],
            yrecv.at[f // F, others, inner(f), :], rs_recv.at[f])
    plans[3 * C] = (3, lambda dst: s1.at[dst], lambda src, d: orecv.at[src], orecv.at[others], x_got.at[3 * C])
    plans[3 * C + 1] = (4, lambda dst: bsend.at[dst], lambda src, d: brecv.at[src], brecv.at[others], x_got.at[3 * C + 1])
    sent = (nsend.at[:, others], rsend.at[:, others], ysend.at[:, others], s1.at[others], bsend.at[others])

    def x_start(kind):
        group, source, target, _, sem = plans[kind]
        for d in order:
            pltpu.make_async_remote_copy(
                src_ref=source(peer(d)), dst_ref=target(h, d),
                send_sem=x_sent.at[group], recv_sem=sem,
                device_id={"hist": peer(d)}, device_id_type=MESH,
            ).start()

    def x_wait(kind):
        local_wait(*plans[kind][3:])

    def near_plan(c):
        bit = 1 if c % 2 == 0 else max(H // 2, 1)
        return bit, [e for e in range(H) if not e & bit]

    def near_copy(c, to, block, target, sem):
        pltpu.make_async_remote_copy(
            src_ref=nsend.at[c, peer(block)], dst_ref=target,
            send_sem=x_sent.at[0], recv_sem=sem,
            device_id={"hist": peer(to)}, device_id_type=MESH,
        ).start()

    def near_start(c):
        bit, rest = near_plan(c)
        for i, e in enumerate(rest):
            near_copy(c, bit, bit | e, nmid.at[c, i], x_got.at[c])

    def near_middle(c):
        bit, rest = near_plan(c)
        local_wait(nmid.at[c], x_got.at[c])
        for i, e in enumerate(rest):
            nsend[c, peer(e)] += nmid[c, i]
        for i, e in enumerate(rest[1:]):
            near_copy(c, e, e, nrecv.at[c, i], x_got.at[2 * C + c])

    def x_sent_wait(group):
        local_wait(sent[group], x_sent.at[group])

    def gap(chip, q):
        return jnp.where(q > chip, q - 1, q)

    def z_copy(g, st, c, q, where):
        block = g.at[2 * q + core, fine(c), :]
        send, recv, target = {
            "partner": (sp, rp, p * 2 + other),
            "in": (sin, rz, t + 2 * inward),
            "out": (sout, rz, t - 2 * inward),
        }[where]
        slot = (partner_slot(st, c // F), q) if where == "partner" else (st, c, gap(target // 2, q))
        return pltpu.make_async_remote_copy(
            src_ref=block, dst_ref=block,
            send_sem=send.at[st], recv_sem=recv.at[slot],
            device_id={"tcol": target}, device_id_type=MESH,
        )

    def partner_slot(st, c):
        return c if st == 0 else C + c // 2

    ahead = rim >= 1 if Z <= 4 else rim >= Z

    def z_partner_wait(g, st, c, n, q):
        step = 1 if st == 0 else 2
        for k in range(c, c + n, step):
            local_wait(g.at[2 * q + other, chunk(k, step), :], rp.at[partner_slot(st, k), q])

    def z_own(g, st, c):
        @pl.when(rim > 0)
        def _():
            z_copy(g, st, c, p, "out").start()

        if Z > 1:
            @pl.when(rim < Z - 1)
            def _():
                z_copy(g, st, c, p, "in").start()

        z_copy(g, st, c, p, "partner").start()

    def exists(side, s):
        return rim < Z - s if side == "in" else rim >= s

    def place(side, s):
        return p + s * inward if side == "in" else p - s * inward

    def z_forward(g, st, side, s, c):
        if s >= (Z if side == "in" else half):
            return

        @pl.when(exists(side, s))
        def _():
            q = place(side, s)
            local_wait(g.at[2 * q + core, fine(c), :], rz.at[st, c, gap(p, q)])
            if side == "in":
                @pl.when(rim > 0)
                def _():
                    z_copy(g, st, c, q, "out").start()
            else:
                z_copy(g, st, c, q, "in").start()
            z_copy(g, st, c, q, "partner").start()

    def z_finish(g, st):
        local_wait(g.at[pl.ds(0, Z)], sp.at[st])
        for k in range(half):
            @pl.when(rim == k)
            def _():
                if k + 1 < Z:
                    local_wait(g.at[pl.ds(0, k + 1)], sin.at[st])
                if k > 0:
                    local_wait(g.at[pl.ds(0, Z - k)], sout.at[st])

    def lane_product(g, acc, b, c, n, first=False):
        at = chunk(c, n)
        m = n * Rc
        high, low = halves(g[b, at, :])
        both = mm(jnp.concatenate([high, low], axis=0), ph[b])
        value = both[:m] + both[m:] + mm(high, plo[b])
        if first:
            acc[at, :] = value
        else:
            acc[at, :] += value

    def use_own(g, st, acc):
        lane_product(g, acc, t, 0, C, True)

    def partner_own(g, st, acc):
        z_partner_wait(g, st, 0, C, p)
        lane_product(g, acc, 2 * p + other, 0, C)

    def use(g, st, acc, side, s, c, n):
        if s >= (Z if side == "in" else half):
            return

        @pl.when(exists(side, s))
        def _():
            lane_product(g, acc, 2 * place(side, s) + core, c, n)

    def partner_use(g, st, acc, side, s, c, n):
        if s >= (Z if side == "in" else half):
            return

        @pl.when(exists(side, s))
        def _():
            q = place(side, s)
            z_partner_wait(g, st, c, n, q)
            lane_product(g, acc, 2 * q + other, c, n)

    def near(c):
        near_sums(c)
        near_start(c)

    def p_half(k):
        for b in range(k * (T // 2), (k + 1) * (T // 2)):
            p_split(b)

    def gather(g, st, acc, steps, actions):
        for step in steps:
            name = step[0]
            if name in ("in", "out"):
                z_forward(g, st, name, step[1], step[2])
            elif name == "own":
                use_own(g, st, acc)
            elif name == "partner":
                partner_own(g, st, acc)
            elif name in ("ahead", "behind"):
                @pl.when(ahead if name == "ahead" else jnp.logical_not(ahead))
                def _():
                    partner_use(g, st, acc, *step[1:])
            elif name == "use":
                use(g, st, acc, *step[1:])
            elif name == "other":
                partner_use(g, st, acc, *step[1:])
            else:
                actions[name](*step[1:])

    def one_steps():
        deep = range(3, Z)
        def hop(s, f):
            yield ("in", s, f)
            if s == 1:
                yield ("out", s, f)

        def far(f):
            for s in deep:
                yield ("in", s, f)

        yield ("begin", 0)
        yield ("near", 0)
        yield ("begin", 1)
        yield ("near", 1)
        yield ("begin", 2)
        yield from hop(1, 0)
        yield ("near", 2)
        yield ("begin", 3)
        yield from hop(1, 1)
        yield ("split", 0)
        yield ("begin", 4)
        yield from hop(1, 2)
        yield ("near", 3)
        yield ("begin", 5)
        yield from hop(2, 0)
        yield ("split", 1)
        yield ("begin", 6)
        yield from hop(1, 3)
        yield from hop(2, 1)
        yield ("begin", 7)
        yield ("own",)
        yield from hop(1, 4)
        yield from hop(2, 2)
        yield from far(0)
        yield from hop(1, 5)
        yield from hop(2, 3)
        yield from far(1)
        yield ("use", "in", 1, 0, 2)
        yield from hop(1, 6)
        yield from hop(2, 4)
        yield from far(2)
        yield ("use", "out", 1, 0, 2)
        yield ("middle", 0)
        yield ("middle", 1)
        yield from hop(1, 7)
        yield ("use", "in", 2, 0, 2)
        yield from hop(2, 5)
        yield from far(3)
        yield ("use", "in", 1, 2, 2)
        yield ("use", "out", 1, 2, 2)
        yield ("partner",)
        for s in range(2, half):
            for f in range(C * F):
                yield ("out", s, f)
            yield ("use", "out", s, 0, C)
            yield ("other", "out", s, 0, C)
        yield from hop(2, 6)
        yield ("middle", 2)
        yield ("middle", 3)
        yield from far(4)
        yield ("other", "in", 1, 0, C)
        yield ("other", "out", 1, 0, C)
        yield ("other", "in", 2, 0, 2)
        yield ("early", 0)
        yield ("early", 1)
        for s in deep:
            yield ("use", "in", s, 0, 2)
        yield from hop(2, 7)
        yield from far(5)
        yield ("use", "in", 2, 2, 2)
        yield ("ahead", "in", 2, 2, 1)
        yield ("early", 2)
        yield ("ahead", "in", 2, 3, 1)
        yield ("early", 3)
        yield from far(6)
        for s in deep:
            yield ("other", "in", s, 0, 2)
        yield ("late", 0)
        yield ("late", 1)
        yield from far(7)
        yield ("behind", "in", 2, 2, 2)
        for c in (2, 3):
            for s in deep:
                yield ("use", "in", s, c, 1)
                yield ("other", "in", s, c, 1)
            yield ("late", c)
        yield ("matrices",)

    def two_steps():
        for c in range(C):
            yield ("begin", c)
        yield ("rest",)
        yield ("drain", 0)
        yield ("own",)
        for f in range(6):
            yield ("in", 1, f)
        yield ("out", 1, 0)
        yield ("in", 1, 6)
        yield ("out", 1, 1)
        yield ("in", 1, 7)
        yield ("out", 1, 2)
        yield ("out", 1, 3)
        yield ("use", "in", 1, 0, C)
        for f in range(4, C * F):
            yield ("in", 2, f - 4)
            yield ("out", 1, f)
        for s in range(2, half):
            for f in range(C * F):
                yield ("out", s, f)
            yield ("use", "out", s, 0, C)
            yield ("other", "out", s, 0, C)
        for f in range(C * F - 4, C * F):
            yield ("in", 2, f)
        yield ("drain", 1)
        deep = range(3, Z)

        def far(f):
            for s in deep:
                yield ("in", s, f)

        yield ("use", "out", 1, 0, C)
        yield from far(0)
        yield ("partner",)
        yield from far(1)
        yield ("other", "in", 1, 0, C)
        yield from far(2)
        yield ("other", "out", 1, 0, C)
        yield ("use", "in", 2, 0, C)
        yield from far(3)
        yield from far(4)
        for s in deep:
            yield ("use", "in", s, 0, 2)
        yield from far(5)
        yield ("other", "in", 2, 0, C)
        yield from far(6)
        yield from far(7)
        for s in deep:
            yield ("use", "in", s, 2, 2)
            yield ("other", "in", s, 0, 2)
        yield ("done", 0)
        yield ("done", 1)
        for s in deep:
            yield ("other", "in", s, 2, 2)
        yield ("done", 2)
        yield ("done", 3)

    for kb in range(nK):
        hist_copy(kb).wait()
        split(hbuf.at[kb], sh.at[kb], sl.at[kb], N, cubic_power, 4)
        if kb == min(1, nK - 1):
            w_split(0, 0)
        if kb + 1 < C:
            w_load(0, kb + 1)
    for kb in range(nK):
        w_step(0, 0, kb)
    for c in range(nK + 1, C):
        w_load(0, c)
    pl.semaphore_wait(barrier, H + 2)
    rs_start(0)
    small[0].start()
    w_load(1, 0)
    small[4].start()
    for c in range(1, C):
        history_sum(0, c)
        rs_start(c)
        w_load(1, c)
    for b in range(nK):
        p_copy(b).start()
    for copy in small[1:4]:
        copy.start()
    small[0].wait()
    small[4].wait()

    def begin_one(f):
        at = inner(f)
        local_wait(rs.at[f // F, :, at, :], rs_recv.at[f])
        total = part[0, f // F, h, at, :] + e1[fine(f), :]
        for d in range(1, H):
            total += rs[f // F, d - 1, at, :]
        pred[fine(f), :] = total
        g1[t, fine(f), :] = cubic_power(total)
        z_own(g1, 0, f)

    def near_sums(c):
        history_sum(1, c)
        part[1, c, h] += e2[chunk(c), :]
        for j in range(H):
            nsend[c, j] = part[1, c, :, :, j * Nh:(j + 1) * Nh]

    def p_split(b):
        p_copy(b).wait()
        split(hbuf.at[b % nK], ph.at[b], plo.at[b], N)
        if b + nK < T:
            p_copy(b + nK).start()

    def split_matrices():
        pltpu.make_async_copy(mat, mat, msem.at[1]).wait()
        split(mat.at[0], ih, il, S)
        split(mat.at[1], kh, kl, S)

        @pl.loop(0, H)
        def _(j):
            for c in range(C):
                at = pl.ds(pl.multiple_of(j * R + c * Rc, Rc), Rc)
                vh[c, j], vl[c, j] = halves(mat[2, at, :])

    def send_right(c):
        value = pred[chunk(c), :] + step_size * acc1[chunk(c), :]
        for j in range(H):
            rsend[c, j] = value[:, j * Nh:(j + 1) * Nh]
        x_start(C + c)
        rf[c, h] = rsend[c, h]

    def early(c):
        @pl.when(ahead)
        def _():
            send_right(c)

    def late(c):
        @pl.when(jnp.logical_not(ahead))
        def _():
            send_right(c)

    gather(g1, 0, acc1, one_steps(), {
        "near": near, "middle": near_middle, "early": early, "late": late, "begin": begin_one, "split": p_half, "matrices": split_matrices, "done": send_right,
    })

    def pair_store(ref, at, value):
        a, b = halves(value)
        ref[at, :Nh] = a
        ref[at, Nh:] = b

    def near_sum():
        for c in range(C):
            if H > 2:
                local_wait(nrecv.at[c], x_got.at[2 * C + c])
            total = nsend[c, h]
            if H > 2:
                for i in range(H // 2 - 1):
                    total += nrecv[c, i]
            s1near[:, chunk(c), :] = total

    for c in range(C):
        x_wait(C + c)
        if c == C // 2 - 1:
            near_sum()
        for j in range(H):
            pair_store(x2, pl.ds(j * R + c * Rc, Rc), rf[c, j])

    def apply(high, low, source):
        wide = mm(high, source[...])
        return wide[:, :Nh] + wide[:, Nh:] + mm(low, source[:, :Nh])

    value = apply(ih[...], il[...], x2)
    s1[...] = value.reshape(H, R, Nh)
    pair_store(q2, pl.ds(0, S), cubic_power(value))

    value = apply(kh[...], kl[...], q2)
    value += s1near[...].reshape(S, Nh)
    pair_store(r2, pl.ds(0, S), step_size * cubic_power(value))
    pair_store(t2, pl.ds(0, S), value)

    for c in range(C):
        value = apply(vh[c].reshape(H * Rc, S), vl[c].reshape(H * Rc, S), r2)
        ysend[c] = value.reshape(H, Rc, Nh)
        for f in range(c * F, c * F + F):
            x_start(("y", f))
        yrecv[c, h] = ysend[c, h]
    for c in range(C):
        value = apply(vh[c].reshape(H * Rc, S), vl[c].reshape(H * Rc, S), t2)
        bsend[:, chunk(c), :] = value.reshape(H, Rc, Nh)

    def begin_two(c):
        for f in range(c * F, c * F + F):
            x_wait(("y", f))
            g2[t, fine(f), :] = jnp.concatenate([yrecv[c, j, inner(f), :] for j in range(H)], axis=1)
            z_own(g2, 1, f)

    def rest():
        zero_ref[...] = jnp.zeros(zero_ref.shape, f32)
        x_start(3 * C)
        orecv[h] = s1[h]
        x_start(3 * C + 1)
        brecv[h] = bsend[h]

    def drain_one():
        local_wait(part.at[0, :, others], rs_send)
        z_finish(g1, 0)
        x_sent_wait(0)
        x_sent_wait(1)

    def drain_two():
        x_wait(3 * C)
        for j in range(H):
            o1_ref[:, j * Nh:(j + 1) * Nh] = orecv[j]
        x_wait(3 * C + 1)
        for group in (2, 3, 4):
            x_sent_wait(group)

    def finish(c):
        at = chunk(c)
        o2_ref[at, :] = acc2[at, :] + jnp.concatenate([brecv[j, at, :] for j in range(H)], axis=1)

    gather(g2, 1, acc2, two_steps(), {
        "begin": begin_two, "rest": rest, "drain": lambda k: (drain_one, drain_two)[k](), "done": finish,
    })
    z_finish(g2, 1)


def shards(*operands):
    history, w1, w2 = operands[:3]
    K, N = history.shape
    S = w1.shape[0]
    H, T, C = lax.axis_size("hist"), lax.axis_size("tcol"), 4
    R = S // H
    Rc, Nh, nK, Z = R // C, N // H, K // N, T // 2
    split_rows = lambda w: w.reshape(H, R, K)
    V, D = pltpu.VMEM, pltpu.SemaphoreType.DMA
    first, second, zero = pl.pallas_call(
        functools.partial(kernel, H, T, C),
        out_shape=[pltpu.VMEM((R, N), f32), pltpu.VMEM((R, N), f32), pltpu.VMEM((1, N), f32)],
        in_specs=[pl.BlockSpec(memory_space=pl.ANY)] * 9,
        out_specs=[pl.BlockSpec(memory_space=pltpu.VMEM)] * 3,
        scratch_shapes=[
            V((nK, N, N), f32), V((2, C, H, Rc, K), f32),
            V((H, Rc, K), bf16), V((H, Rc, K), bf16),
            V((nK, N, N), bf16), V((nK, N, N), bf16),
            V((T, N, N), bf16), V((T, N, N), bf16),
            V((3, S, S), f32),
            *[V((S, S), bf16)] * 4, *[V((C, H, Rc, S), bf16)] * 2,
            V((R, N), f32), V((R, N), f32),
            V((2, C, H, Rc, N), f32), V((C, H - 1, Rc, N), f32),
            V((R, N), f32), V((R, N), f32), V((R, N), f32),
            V((T, R, N), f32), V((T, R, N), f32),
            V((C, H, H, Rc, Nh), f32), V((C, H // 2, H, Rc, Nh), f32), V((C, max(H // 2 - 1, 1), H, Rc, Nh), f32),
            V((C, H, Rc, Nh), f32), V((C, H, Rc, Nh), f32),
            V((H, R, Nh), f32), V((H, R, Nh), f32),
            V((C, H, Rc, Nh), f32), V((C, H, Rc, Nh), f32),
            V((H, R, Nh), f32), V((H, R, Nh), f32), V((H, R, Nh), f32),
            *[V((S, 2 * Nh), bf16)] * 4,
            D((nK,)), D((C,)), D((3,)),
            D, D((2 * C,)), D((5,)), D((3 * C + 2,)),
            D((2,)), D((2,)), D((2,)), D((2, 2 * C, max(Z - 1, 1))), D((C + C // 2, Z)),
        ],
        compiler_params=pltpu.CompilerParams(
            collective_id=0, has_side_effects=True, vmem_limit_bytes=63 * 1024 * 1024
        ),
    )(history, split_rows(w1), split_rows(w2), *operands[3:])
    return first + zero, second + zero


def solution(mesh):
    return jax.shard_map(
        shards,
        mesh=mesh,
        in_specs=(
            P("hist", "tcol"),
            P(None, "hist"),
            P(None, "hist"),
            P(),
            P(None, "tcol"),
            P(),
            P(),
            P(None, "tcol"),
            P(None, "tcol"),
        ),
        out_specs=(P("hist", "tcol"), P("hist", "tcol")),
        check_vma=False,
    )
```
